32 devices in a mesh: grp: 4 (over y, x), dom: 8 (over z, core).
Axes of the slice: x: 2, y: 2, z: 4, core: 2. Of those that a mesh axis runs over, the one named last changes fastest.
Arguments:
- u_int: bfloat16 [16384, 192], P(('grp', 'dom')), may hold values from -1.59375 to 1.59375
- u_if: bfloat16 [5632, 192], P('dom'), may hold values from -1.59375 to 1.59375
- load_int: float32 [16384, 192], P(('grp', 'dom')), may hold values from -6 to 6
- load_if: float32 [5632, 192], P('dom'), may hold values from -6 to 6
- conn: int32 [65536, 8], P(('grp', 'dom')), may hold values from 0 to 1343
- send_map: int32 [128, 32], P(('grp', 'dom')), may hold values from 0 to 1215
- counts: int32 [32], P(('grp', 'dom')), may hold values from 256 to 2048, as said below
- elem_size: float32 [65536], P(('grp', 'dom')), may hold values from 0.7 to 1.4
- stiffness: float32 [65536], P(('grp', 'dom')), may hold values from 0.5 to 2
- yield_stress: float32 [65536], P(('grp', 'dom')), may hold values from 0.5 to 2
- relax_rate: float32 [65536], P(('grp', 'dom')), may hold values from 0.02 to 0.5
- stress_init: float32 [48, 65536], P(None, ('grp', 'dom')), may hold values from -6 to 6
- kinv_int: bfloat16 [49152, 1536], P(('grp', 'dom')), may hold values from -0.15625 to 0.15625
- sinv: bfloat16 [16896, 16896], P('grp', 'dom'), may hold values from -0.0625 to 0.0625
Outputs:
- du_int: float32 [16384, 192], P(('grp', 'dom'))
- du_if: float32 [5632, 192], P(('grp', 'dom'))
- stress_end: float32 [48, 65536], P(None, ('grp', 'dom'))
The draws below stay inside these ranges and needn't reach their ends.
Inputs may be any that keep to these rules, and one draw needn't show every extreme that they name: `counts`: every partition has at least 256 live elements and some partition has exactly 2048.
All inputs are finite; a program needn't handle non-finite values.
Results may differ from the reference program's by a relative error of at most 0.0046.
Values may be sent and summed in bfloat16 or wider, within the bound.
No kernel may reach another device: no remote copies, remote signals or barrier semaphores. Data moves between devices by JAX's collectives and lax.ppermute only.
A program may use at most 128 MiB of HBM per device.

```python
import math
import jax
import jax.numpy as jnp
import numpy as np
from jax import lax

FOURIER = 64
TIMES = 32
INT_NODES = 512
IF_NODES = 5632
ELEM_DEV = 2048
SLOT = 32
HOP = 2
STRESS_ROWS = 48
NBR = 4
PARTITIONS = 32
ELEMS = 65536
NODES = 16384
INT_DOF = 1536
IF_DOF = 16896
LOCAL = 1216
BUFFER = 1344
N_GRP = 4
N_DOM = 8


def draw_counts(key, part):
    keys = jax.random.split(jax.random.fold_in(key, 7), 4)
    base = jax.random.randint(keys[0], (PARTITIONS,), ELEM_DEV // 8, ELEM_DEV // 2 + 1)
    heavy = jax.random.randint(keys[1], (PARTITIONS,), 3 * ELEM_DEV // 4, ELEM_DEV + 1)
    choose = jax.random.randint(keys[2], (PARTITIONS,), 0, 8)
    fullest = jax.random.randint(keys[3], (), 0, PARTITIONS)
    result = jnp.where(choose == 0, heavy, base)
    result = jnp.where(jnp.arange(PARTITIONS) == fullest, ELEM_DEV, result)
    return result.astype(jnp.int32)


def place_ends(entries, key, low, largest):
    longest = entries.shape.index(max(entries.shape))
    spots = []
    for shift in (0, 1):
        where = [jax.random.randint(jax.random.fold_in(key, axis), (), 0, length) for axis, length in enumerate(entries.shape)]
        where[longest] = (where[longest] + shift) % entries.shape[longest]
        spots.append(tuple(where))
    return entries.at[spots[0]].set(low).at[spots[1]].set(largest)


def strengthened(array, key, source, target, shards_of, factor):
    def block_of(dim):
        return (jnp.arange(array.shape[dim]) // (array.shape[dim] // shards_of)).reshape((-1,) + (1,) * (array.ndim - 1 - dim))

    near = jax.random.permutation(key, shards_of)[block_of(target)]
    other_side = (block_of(target) + shards_of // 2) % shards_of
    return jnp.where((block_of(source) == near) | (block_of(source) == other_side), factor * array, array)


def level_of(own_key, extent, cuts, least, largest):
    def one(dim, blocks):
        draws = jax.random.uniform(jax.random.fold_in(jax.random.fold_in(own_key, 6), dim), (blocks,), jnp.float32, least / len(cuts), largest / len(cuts))
        return jnp.repeat(jnp.exp(draws), extent[dim] // blocks).reshape((-1,) + (1,) * (len(extent) - dim - 1))

    level = one(*cuts[0])
    for cut in cuts[1:]:
        level = level * one(*cut)
    return level


def scatter_about(rng, shape, deviation, most, cuts=(), kind=jnp.bfloat16):
    factor_of = level_of(rng, shape, cuts, -0.22, 0.18) if cuts else 1.0
    values = jax.random.normal(rng, shape, jnp.float32) * deviation * factor_of
    return jnp.minimum(jnp.maximum(values, -most), most).astype(kind)


def heavy_noise(stream_key, dims, scale, most, cuts, heavy, held_as=jnp.bfloat16):
    entries = scale * jax.random.normal(stream_key, dims, jnp.float32)
    if cuts:
        entries = entries * level_of(stream_key, dims, cuts, -0.22, 0.18)
    return jnp.clip(strengthened(entries, jax.random.fold_in(stream_key, 3), *heavy), -most, most).astype(held_as)


def setup_inputs(seed: int = 0) -> dict:
    arg_keys = jax.random.split(jax.random.key(seed), 15)
    u_int = scatter_about(arg_keys[0], (NODES, 3 * FOURIER), 0.2, 1.59375, ((0, 32),))
    u_if = scatter_about(arg_keys[1], (IF_NODES, 3 * FOURIER), 0.2, 1.59375, ((0, 8),))
    load_int = scatter_about(arg_keys[2], (NODES, 3 * FOURIER), 1.0, 6.0, ((0, 32),), jnp.float32)
    load_if = scatter_about(arg_keys[3], (IF_NODES, 3 * FOURIER), 1.0, 6.0, ((0, 8),), jnp.float32)
    conn = place_ends(jax.random.randint(arg_keys[4], (ELEMS, 8), 0, BUFFER), jax.random.fold_in(arg_keys[4], 1), 0, BUFFER - 1).astype(jnp.int32)
    send_map = place_ends(jax.random.randint(arg_keys[5], (PARTITIONS * NBR, SLOT), 0, LOCAL), jax.random.fold_in(arg_keys[5], 1), 0, LOCAL - 1).astype(jnp.int32)
    counts = draw_counts(jax.random.fold_in(arg_keys[14], 71), 0)
    elem_size = jnp.clip(jnp.exp(math.log(1.4) - 0.6931472 * jax.random.uniform(arg_keys[7], (ELEMS,), jnp.float32) ** level_of(arg_keys[7], (ELEMS,), ((0, 32),), -0.2, 0.2)), 0.7, 1.4)
    stiffness = jnp.clip(jnp.exp(math.log(2.0) - 1.3862944 * jax.random.uniform(arg_keys[8], (ELEMS,), jnp.float32) ** level_of(arg_keys[8], (ELEMS,), ((0, 32),), -0.2, 0.2)), 0.5, 2.0)
    yield_stress = jnp.clip(jnp.exp(math.log(2.0) - 1.3862944 * jax.random.uniform(arg_keys[9], (ELEMS,), jnp.float32) ** level_of(arg_keys[9], (ELEMS,), ((0, 32),), -0.2, 0.2)), 0.5, 2.0)
    relax_rate = jnp.clip(jnp.exp(math.log(0.5) - 3.218876 * jax.random.uniform(arg_keys[10], (ELEMS,), jnp.float32) ** level_of(arg_keys[10], (ELEMS,), ((0, 32),), -0.2, 0.2)), 0.02, 0.5)
    stress_init = scatter_about(arg_keys[11], (STRESS_ROWS, ELEMS), 1.0, 6.0, ((1, 32),), jnp.float32)
    kinv_int = scatter_about(arg_keys[12], (PARTITIONS * INT_DOF, INT_DOF), INT_DOF ** -0.5, 0.15625, ((0, 32),))
    sinv = heavy_noise(arg_keys[13], (IF_DOF, IF_DOF), IF_DOF ** -0.5, 0.0625, ((0, 4), (1, 8)), (1, 0, 8, 2.0))
    return {"u_int": u_int, "u_if": u_if, "load_int": load_int, "load_if": load_if, "conn": conn, "send_map": send_map, "counts": counts, "elem_size": elem_size, "stiffness": stiffness, "yield_stress": yield_stress, "relax_rate": relax_rate, "stress_init": stress_init, "kinv_int": kinv_int, "sinv": sinv}


POISSON = 0.3
HIGHEST = lax.Precision.HIGHEST

def strain_table():
    gauss = 1.0 / math.sqrt(3.0)
    table = np.zeros((6, 8, 8, 3))
    for point in range(8):
        coords = [((point >> bit & 1) * 2 - 1) * gauss for bit in range(3)]
        for corner in range(8):
            signs = [(corner >> bit & 1) * 2 - 1 for bit in range(3)]
            deriv = []
            for axis in range(3):
                value = signs[axis] / 8.0
                for other in range(3):
                    if other != axis:
                        value = value * (1.0 + signs[other] * coords[other])
                deriv.append(value)
            table[0, point, corner, 0] = deriv[0]
            table[1, point, corner, 1] = deriv[1]
            table[2, point, corner, 2] = deriv[2]
            table[3, point, corner, 0] = deriv[1]
            table[3, point, corner, 1] = deriv[0]
            table[4, point, corner, 1] = deriv[2]
            table[4, point, corner, 2] = deriv[1]
            table[5, point, corner, 2] = deriv[0]
            table[5, point, corner, 0] = deriv[2]
    return jnp.asarray(table.reshape(48, 24), jnp.float32).astype(jnp.bfloat16)

def time_tables(times, fourier):
    theta = 2.0 * math.pi * (np.arange(times) + 0.3) / times
    synthesis = np.zeros((fourier, times))
    for column in range(fourier):
        harmonic = column // 2
        if column % 2 == 0:
            synthesis[column] = np.cos(harmonic * theta)
        else:
            synthesis[column] = np.sin((harmonic + 1) * theta)
    analysis = synthesis.T * (2.0 / times)
    analysis[:, 0] = 1.0 / times
    return (jnp.asarray(synthesis, jnp.float32), jnp.asarray(analysis, jnp.float32))

def element_update(rows, conn_dev, count, size_e, stiff_e, yield_e, rate_e, stress_zero):
    table = strain_table()
    fourier = rows.shape[1] // 3
    synthesis, analysis = time_tables(TIMES, fourier)
    elems = conn_dev.shape[0]
    gathered = jnp.take(rows, conn_dev.reshape(-1), axis=0).reshape(elems, 24, fourier)
    strain_hat = jnp.einsum('qk,ekf->qfe', table.astype(jnp.float32), gathered.astype(jnp.float32), precision=HIGHEST)
    strain = jnp.einsum('qfe,fm->mqe', strain_hat, synthesis, precision=HIGHEST) * (2.0 / size_e)
    delta = strain - jnp.roll(strain, 1, axis=0)
    lame_first = POISSON / ((1.0 + POISSON) * (1.0 - 2.0 * POISSON))
    shear_mod = 1.0 / (2.0 * (1.0 + POISSON))
    coef = jnp.asarray(np.concatenate([np.full(24, 2.0 * shear_mod), np.full(24, shear_mod)]).reshape(48, 1), jnp.float32)

    def advance(stress, step_delta):
        trace = step_delta[0:8] + step_delta[8:16] + step_delta[16:24]
        volume = jnp.concatenate([trace, trace, trace, jnp.zeros_like(step_delta[24:48])], axis=0)
        increment = coef * step_delta + lame_first * volume
        stress = stress + stiff_e * increment - rate_e * yield_e * jnp.tanh(stress / yield_e)
        return (stress, stress)
    final, history = lax.scan(advance, stress_zero, delta, unroll=8)
    live = (jnp.arange(elems) < count).astype(jnp.float32)
    stress_hat = jnp.einsum('mqe,mf->qfe', history, analysis, precision=HIGHEST)
    forces = jnp.einsum('qfe,qk->ekf', stress_hat, table.astype(jnp.float32), precision=HIGHEST)
    forces = forces * (size_e * size_e * 0.25 * live)[:, None, None]
    assembled = jax.ops.segment_sum(forces.reshape(elems * 8, 3 * fourier), conn_dev.reshape(-1), num_segments=rows.shape[0])
    return (final * live, assembled)

def reference(u_int, u_if, load_int, load_if, conn, send_map, counts, elem_size, stiffness, yield_stress, relax_rate, stress_init, kinv_int, sinv):
    width = 3 * FOURIER
    parts = N_GRP * N_DOM
    if_dev = IF_NODES // N_DOM
    offsets = list(range(-HOP, 0)) + list(range(1, HOP + 1))
    own_if = jnp.broadcast_to(u_if.reshape(1, N_DOM, if_dev, width), (N_GRP, N_DOM, if_dev, width))
    local = jnp.concatenate([u_int.reshape(N_GRP, N_DOM, INT_NODES, width), own_if], axis=2)
    smap = send_map.reshape(N_GRP, N_DOM, NBR, SLOT)

    def pick_rows(rows, index):
        return jnp.take(rows, index.reshape(-1), axis=0).reshape(NBR, SLOT, width)
    blocks = jax.vmap(jax.vmap(pick_rows))(local, smap)
    halo = jnp.stack([jnp.roll(blocks[:, :, slot_index], offsets[slot_index], axis=1) for slot_index in range(NBR)], axis=2)
    buffers = jnp.concatenate([local, halo.reshape(N_GRP, N_DOM, NBR * SLOT, width)], axis=2).reshape(parts, BUFFER, width)

    def one_part(inputs):
        rows, conn_dev, count, size_e, stiff_e, yield_e, rate_e, stress_zero = inputs
        return element_update(rows, conn_dev, count, size_e, stiff_e, yield_e, rate_e, stress_zero)
    stress_parts, assembled = lax.map(one_part, (buffers, conn.reshape(parts, ELEM_DEV, 8), counts, elem_size.reshape(parts, ELEM_DEV), stiffness.reshape(parts, ELEM_DEV), yield_stress.reshape(parts, ELEM_DEV), relax_rate.reshape(parts, ELEM_DEV), jnp.transpose(stress_init.reshape(STRESS_ROWS, parts, ELEM_DEV), (1, 0, 2))))
    assembled = assembled.reshape(N_GRP, N_DOM, BUFFER, width)
    owned = assembled[:, :, :LOCAL]
    back = assembled[:, :, LOCAL:].reshape(N_GRP, N_DOM, NBR, SLOT, width)
    returned = jnp.stack([jnp.roll(back[:, :, slot_index], -offsets[slot_index], axis=1) for slot_index in range(NBR)], axis=2)

    def add_back(values, index):
        return jax.ops.segment_sum(values.reshape(NBR * SLOT, width), index.reshape(-1), num_segments=LOCAL)
    owned = owned + jax.vmap(jax.vmap(add_back))(returned, smap)
    r_int = load_int - owned[:, :, :INT_NODES].reshape(NODES, width)
    r_if = load_if - lax.optimization_barrier(jnp.sum(owned[:, :, INT_NODES:], axis=0)).reshape(IF_NODES, width)
    rhs_int = r_int.astype(jnp.bfloat16)
    rhs_if = r_if.astype(jnp.bfloat16)

    def one_solve(inputs):
        block, rhs = inputs
        return jnp.dot(block, rhs.reshape(INT_DOF, FOURIER), preferred_element_type=jnp.float32).reshape(INT_NODES, width)
    du_int = lax.map(one_solve, (kinv_int.reshape(parts, INT_DOF, INT_DOF), rhs_int.reshape(parts, INT_NODES, width)))
    du_int = du_int.reshape(NODES, width)
    du_if = jnp.dot(sinv, rhs_if.reshape(IF_DOF, FOURIER), preferred_element_type=jnp.float32).reshape(IF_NODES, width)
    stress_end = jnp.transpose(stress_parts, (1, 0, 2)).reshape(STRESS_ROWS, ELEMS)
    return (du_int, du_if, stress_end)
```

```python
import functools
import math

import jax
import jax.numpy as jnp
import numpy as np
from jax import lax
from jax.experimental import pallas as pl
from jax.experimental.pallas import tpu as pltpu
from jax.sharding import PartitionSpec as P

TIMES = 32
POISSON = 0.3
LAME = POISSON / ((1.0 + POISSON) * (1.0 - 2.0 * POISSON))
SHEAR = 1.0 / (2.0 * (1.0 + POISSON))
HIGHEST = lax.Precision.HIGHEST
STEPS = 8
GROUPS = TIMES // STEPS
ROWS = 3 * TIMES
NT = (((1,), (1,)), ((), ()))
BF16 = jnp.bfloat16
F32 = jnp.float32


def strain_table():
    gauss = 1.0 / math.sqrt(3.0)
    table = np.zeros((6, 8, 8, 3))
    for point in range(8):
        coords = [((point >> bit & 1) * 2 - 1) * gauss for bit in range(3)]
        for corner in range(8):
            signs = [(corner >> bit & 1) * 2 - 1 for bit in range(3)]
            deriv = []
            for axis in range(3):
                value = signs[axis] / 8.0
                for other in range(3):
                    if other != axis:
                        value = value * (1.0 + signs[other] * coords[other])
                deriv.append(value)
            table[0, point, corner, 0] = deriv[0]
            table[1, point, corner, 1] = deriv[1]
            table[2, point, corner, 2] = deriv[2]
            table[3, point, corner, 0] = deriv[1]
            table[3, point, corner, 1] = deriv[0]
            table[4, point, corner, 1] = deriv[2]
            table[4, point, corner, 2] = deriv[1]
            table[5, point, corner, 2] = deriv[0]
            table[5, point, corner, 0] = deriv[2]
    return table.reshape(48, 24).astype(np.float32)


def time_tables(fourier):
    theta = 2.0 * math.pi * (np.arange(TIMES) + 0.3) / TIMES
    synthesis = np.zeros((fourier, TIMES))
    for column in range(fourier):
        harmonic = column // 2
        if column % 2 == 0:
            synthesis[column] = np.cos(harmonic * theta)
        else:
            synthesis[column] = np.sin((harmonic + 1) * theta)
    analysis = synthesis.T * (2.0 / TIMES)
    analysis[:, 0] = 1.0 / TIMES
    return synthesis.astype(np.float32), analysis.astype(np.float32)


def constants(fourier):
    synthesis, analysis = time_tables(fourier)
    differences = synthesis.astype(np.float64) - np.roll(synthesis.astype(np.float64), 1, axis=1)
    synth = np.zeros((GROUPS, 3, STEPS, 3, fourier))
    anal = np.zeros((GROUPS, 3, STEPS, 3, fourier))
    for comp in range(3):
        synth[:, comp, :, comp, :] = differences.T.reshape(GROUPS, STEPS, fourier)
        anal[:, comp, :, comp, :] = analysis.reshape(GROUPS, STEPS, fourier)
    synth = synth.reshape(ROWS, 3 * fourier).astype(np.float32)
    table = strain_table().reshape(48, 8, 3)
    strain = np.zeros((STEPS, 48, 8, 2, 3, STEPS), np.float32)
    force = np.zeros((8, 3, STEPS, STEPS, 48), np.float32)
    for step in range(STEPS):
        for half in range(2):
            strain[step, :, :, half, :, step] = table
        force[:, :, step, step, :] = table.transpose(1, 2, 0)
    high = jnp.asarray(synth).astype(BF16)
    low = (jnp.asarray(synth) - high.astype(F32)).astype(BF16)
    return (
        high,
        low,
        jnp.asarray(strain.reshape(STEPS * 48, 16 * 3 * STEPS)).astype(BF16),
        jnp.asarray(force.reshape(24 * STEPS, STEPS * 48)).astype(BF16),
        jnp.asarray(anal.reshape(ROWS, 3 * fourier), F32),
    )


def up(n, to):
    return -(-n // to) * to


def element_kernel(
    count_ref, int_ref, if_ref, *refs, neighbours, chunk, own, padded
):
    halo_refs = refs[:neighbours]
    conn_ref, par_ref, init_ref, high_ref, low_ref, strain_ref, force_ref = refs[neighbours : neighbours + 7]
    end_ref, pint_ref, pif_ref, back_ref, nodes, onehot, corners, forces, history, total = refs[neighbours + 7 :]
    index = pl.program_id(0)
    n_int, n_if, slots = int_ref.shape[0], if_ref.shape[0], halo_refs[0].shape[0]
    halo_at = up(own, 128)

    @pl.when(index == 0)
    def _():
        nodes[...] = jnp.zeros_like(nodes)
        halo = jnp.concatenate([ref[...].astype(F32) for ref in halo_refs], axis=0).astype(BF16)
        pieces = ((0, n_int, int_ref[...]), (n_int, n_if, if_ref[...]), (halo_at, neighbours * slots, halo))
        for start, length, rows in pieces:
            value = lax.dot_general(high_ref[...], rows, NT, preferred_element_type=F32)
            value = value + lax.dot_general(low_ref[...], rows, NT, preferred_element_type=F32)
            upper = value.astype(BF16).astype(F32)
            lower = value - upper
            for group in range(GROUPS):
                part = slice(group * 3 * STEPS, (group + 1) * 3 * STEPS)
                nodes[group * 6 * STEPS : (group + 1) * 6 * STEPS, start : start + length] = jnp.concatenate(
                    [upper[part], lower[part]], axis=0
                ).astype(BF16)
        total[...] = jnp.zeros_like(total)

    live = index * chunk < count_ref[0]

    @pl.when(jnp.logical_not(live))
    def _():
        end_ref[...] = jnp.zeros_like(end_ref)

    @pl.when(live)
    def _():
        @pl.loop(0, 8)
        def _(corner):
            node = conn_ref[pl.ds(corner, 1), :]
            node = node + jnp.where(node >= own, halo_at - own, 0)
            hot = jnp.where(lax.broadcasted_iota(jnp.int32, (padded, chunk), 0) == node, 1.0, 0.0).astype(BF16)
            onehot[corner] = hot
            found = jnp.dot(nodes[...], hot, preferred_element_type=F32).astype(BF16)
            rows = pl.ds(pl.multiple_of(corner * 6 * STEPS, 16), 6 * STEPS)
            for group in range(GROUPS):
                corners[group, rows, :] = found[group * 6 * STEPS : (group + 1) * 6 * STEPS]

        size, limit, rate = par_ref[0:1, :], par_ref[2:3, :], par_ref[3:4, :]
        modulus = par_ref[1:2, :] * (2.0 / size)

        def wide(row):
            return jnp.broadcast_to(row, (8, chunk))

        twice_shear, shear, lame = wide(modulus * (2.0 * SHEAR)), wide(modulus * SHEAR), wide(modulus * LAME)
        inverse, relax = wide(1.0 / limit), wide(rate * limit)
        slot = index * chunk + lax.broadcasted_iota(jnp.int32, (1, chunk), 1)
        alive = jnp.where(slot < count_ref[0], 1.0, 0.0)
        scale = jnp.broadcast_to(size * size * 0.25 * alive, (3 * STEPS, chunk))

        def advance(group, stress):
            delta = jnp.dot(strain_ref[...], corners[group], preferred_element_type=F32)
            for step in range(STEPS):
                d = [delta[step * 48 + comp * 8 : step * 48 + comp * 8 + 8] for comp in range(6)]
                trace = lame * (d[0] + d[1] + d[2])
                stress = tuple(
                    s
                    + (twice_shear * d[comp] + trace if comp < 3 else shear * d[comp])
                    - relax * jnp.tanh(s * inverse)
                    for comp, s in enumerate(stress)
                )
                history[step * 48 : (step + 1) * 48, :] = jnp.concatenate(stress, axis=0).astype(BF16)
            force = jnp.dot(force_ref[...], history[...], preferred_element_type=F32)
            rows = pl.ds(pl.multiple_of(group * 3 * STEPS, 8), 3 * STEPS)
            for corner in range(8):
                part = force[corner * 3 * STEPS : (corner + 1) * 3 * STEPS]
                forces[rows, corner * chunk : (corner + 1) * chunk] = part * scale
            return stress

        stress = tuple(init_ref[comp * 8 : comp * 8 + 8, :] for comp in range(6))
        stress = lax.fori_loop(0, GROUPS, advance, stress)
        for comp in range(6):
            end_ref[comp * 8 : comp * 8 + 8, :] = stress[comp] * alive
        half = padded // 2

        @pl.loop(0, 2)
        def _(block):
            rows = pl.ds(pl.multiple_of(block * half, 16), half)
            sums = None
            for corner in range(8):
                part = forces[:, corner * chunk : (corner + 1) * chunk].astype(BF16)
                term = lax.dot_general(onehot[corner, rows, :], part, NT, preferred_element_type=F32)
                sums = term if sums is None else sums + term
            total[rows, :] += sums

    @pl.when(index == pl.num_programs(0) - 1)
    def _():
        pint_ref[...] = total[:n_int]
        pif_ref[...] = total[n_int:own]
        for slot_index in range(neighbours):
            start = halo_at + slot_index * slots
            back_ref[slot_index] = total[start : start + slots]


def whole(shape):
    return pl.BlockSpec(shape, lambda *_: (0,) * len(shape))


def element_phase(u_int, u_if, halos, conn, count, params, stress_init, tables):
    elems = conn.shape[1]
    chunk = 256
    own = u_int.shape[0] + u_if.shape[0]
    neighbours, slots = len(halos), halos[0].shape[0]
    padded = up(own, 128) + up(neighbours * slots, 128)
    n_rows = stress_init.shape[0]

    def columns(rows):
        return pl.BlockSpec((rows, chunk), lambda c, *_: (0, c))

    synth_high, synth_low, strain, force = tables[:4]
    return pl.pallas_call(
        functools.partial(element_kernel, neighbours=neighbours, chunk=chunk, own=own, padded=padded),
        grid_spec=pltpu.PrefetchScalarGridSpec(
            num_scalar_prefetch=1,
            grid=(elems // chunk,),
            in_specs=[whole(u_int.shape), whole(u_if.shape)]
            + [whole(h.shape) for h in halos]
            + [columns(8), columns(4), columns(n_rows)]
            + [whole(t.shape) for t in tables[:4]],
            out_specs=[
                columns(n_rows),
                whole((u_int.shape[0], ROWS)),
                whole((u_if.shape[0], ROWS)),
                whole((neighbours, slots, ROWS)),
            ],
            scratch_shapes=[
                pltpu.VMEM((2 * ROWS, padded), BF16),
                pltpu.VMEM((8, padded, chunk), BF16),
                pltpu.VMEM((GROUPS, 48 * STEPS, chunk), BF16),
                pltpu.VMEM((ROWS, 8 * chunk), F32),
                pltpu.VMEM((48 * STEPS, chunk), BF16),
                pltpu.VMEM((padded, ROWS), F32),
            ],
        ),
        out_shape=[
            jax.ShapeDtypeStruct(stress_init.shape, F32),
            jax.ShapeDtypeStruct((u_int.shape[0], ROWS), F32),
            jax.ShapeDtypeStruct((u_if.shape[0], ROWS), F32),
            jax.ShapeDtypeStruct((neighbours, slots, ROWS), F32),
        ],
        compiler_params=pltpu.CompilerParams(vmem_limit_bytes=32 << 20),
        name="elements",
    )(count, u_int, u_if, *halos, conn, params, stress_init, *tables[:4])


def added_back(own, map_ref, returned, first):
    for slot_index, ref in enumerate(returned):
        hot = (
            lax.broadcasted_iota(jnp.int32, (own.shape[0], ref.shape[0]), 0) + first
            == map_ref[slot_index : slot_index + 1, :]
        )
        hot = jnp.where(hot, 1.0, 0.0).astype(BF16)
        value = ref[...]
        high = value.astype(BF16)
        low = (value - high.astype(F32)).astype(BF16)
        own = own + jnp.dot(hot, high, preferred_element_type=F32) + jnp.dot(hot, low, preferred_element_type=F32)
    return own


def interface_kernel(own_ref, map_ref, *refs, first):
    returned, (a_ref, b_ref) = refs[:-2], refs[-2:]
    value = added_back(own_ref[...], map_ref, returned, first)
    half = a_ref.shape[0]
    a_ref[...] = value[:half]
    b_ref[...] = value[half:]


def interleaved(value, scratch):
    nodes, width = value.shape
    fourier = width // 3
    for comp in range(3):
        scratch[pl.ds(comp, nodes, stride=3), :] = value[:, comp * fourier : (comp + 1) * fourier]
    return scratch[...]


def separated(value, scratch):
    scratch[...] = value
    nodes = value.shape[0] // 3
    return jnp.concatenate([scratch[pl.ds(comp, nodes, stride=3), :] for comp in range(3)], axis=1)


def interior_kernel(own_ref, map_ref, *refs):
    returned = refs[:-6]
    load_ref, anal_ref, kinv_ref, du_ref, scratch, _ = refs[-6:]
    value = added_back(own_ref[...], map_ref, returned, 0)
    force = jnp.dot(value, anal_ref[...], precision=HIGHEST, preferred_element_type=F32)
    rhs = interleaved(load_ref[...] - force, scratch).astype(BF16)
    du = jnp.dot(kinv_ref[...], rhs, preferred_element_type=F32)
    du_ref[...] = separated(du, scratch)


def rhs_kernel(load_ref, own_a, got_a, own_b, got_b, anal_ref, rhs_ref, scratch):
    half = own_a.shape[0]
    total = jnp.concatenate([own_a[...] + got_a[...], own_b[...] + got_b[...]], axis=0)
    force = jnp.dot(total, anal_ref[...], precision=HIGHEST, preferred_element_type=F32)
    rhs_ref[...] = interleaved(load_ref[...] - force, scratch).astype(BF16)


def solve_kernel(order_ref, sinv_ref, rhs_ref, out_ref):
    value = jnp.dot(sinv_ref[0], rhs_ref[...], preferred_element_type=F32)
    half = value.shape[0] // 2
    out_ref[0] = jnp.concatenate([value[:half], value[half:]], axis=1).astype(out_ref.dtype)


def solve_blocks(order, sinv, rhs, peers, dtype):
    rows = sinv.shape[0] // peers
    fourier = rhs.shape[1]
    count = order.shape[0]
    return pl.pallas_call(
        solve_kernel,
        grid_spec=pltpu.PrefetchScalarGridSpec(
            num_scalar_prefetch=1,
            grid=(count,),
            in_specs=[
                pl.BlockSpec((1, rows, sinv.shape[1]), lambda j, order: (order[j], 0, 0)),
                whole(rhs.shape),
            ],
            out_specs=pl.BlockSpec((1, rows // 2, 2 * fourier), lambda j, order: (j, 0, 0)),
        ),
        out_shape=jax.ShapeDtypeStruct((count, rows // 2, 2 * fourier), dtype),
        cost_estimate=pl.CostEstimate(
            flops=2 * count * rows * sinv.shape[1] * fourier,
            bytes_accessed=2 * count * rows * sinv.shape[1],
            transcendentals=0,
        ),
        name="interface_solve",
    )(order, sinv.reshape(peers, rows, sinv.shape[1]), rhs)


def last_kernel(mine_ref, got_ref, out_ref, scratch):
    value = mine_ref[0] + got_ref[0].astype(F32)
    half = value.shape[0]
    fourier = value.shape[1] // 2
    out_ref[...] = separated(jnp.concatenate([value[:, :fourier], value[:, fourier:]], axis=0), scratch)


def swapped(shard, axis, bit):
    peers = lax.axis_size(axis)
    return lax.ppermute(shard, axis, [(i, i ^ bit) for i in range(peers)])


def passed_along(shard, axis, by):
    peers = lax.axis_size(axis)
    return lax.ppermute(shard, axis, [(i, (i + by) % peers) for i in range(peers)])


def per_device(
    u_int,
    u_if,
    load_int,
    load_if,
    conn,
    send_map,
    counts,
    elem_size,
    stiffness,
    yield_stress,
    relax_rate,
    stress_init,
    kinv_int,
    sinv,
):
    width = u_int.shape[1]
    fourier = width // 3
    n_int, n_if = u_int.shape[0], u_if.shape[0]
    neighbours, slots = send_map.shape
    reach = neighbours // 2
    offsets = list(range(-reach, 0)) + list(range(1, reach + 1))
    tables = constants(fourier)
    analysis = tables[4]

    local = jnp.concatenate([u_int, u_if], axis=0)
    blocks = jnp.take(local, send_map.reshape(-1), axis=0).reshape(neighbours, slots, width)
    halos = [passed_along(blocks[j], "dom", offsets[j]) for j in range(neighbours)]
    params = jnp.stack([elem_size, stiffness, yield_stress, relax_rate], axis=0)
    stress_end, p_int, p_if, back = element_phase(
        u_int, u_if, halos, conn.T, counts, params, stress_init, tables
    )
    returned = [passed_along(back[j], "dom", -offsets[j]) for j in range(neighbours)]

    half = n_if // 2
    part_a, part_b = pl.pallas_call(
        functools.partial(interface_kernel, first=n_int),
        out_shape=[jax.ShapeDtypeStruct((half, ROWS), F32), jax.ShapeDtypeStruct((n_if - half, ROWS), F32)],
        name="interface_forces",
    )(p_if, send_map, *returned)

    bits = [1 << b for b in range(lax.axis_size("grp").bit_length() - 1)]
    got_a = got_b = None
    for bit_a, bit_b in zip(bits, bits[::-1]):
        if got_a is not None:
            part_a, part_b = part_a + got_a, part_b + got_b
        got_a, got_b = swapped(part_a, "grp", bit_a), swapped(part_b, "grp", bit_b)

    du_int = pl.pallas_call(
        interior_kernel,
        out_shape=jax.ShapeDtypeStruct((n_int, width), F32),
        scratch_shapes=[pltpu.VMEM((3 * n_int, fourier), F32), pltpu.VMEM((8, 128), F32)],
        cost_estimate=pl.CostEstimate(
            flops=2 * kinv_int.size * fourier, bytes_accessed=2 * kinv_int.size, transcendentals=0
        ),
        name="interior_solve",
    )(p_int, send_map, *returned, load_int, analysis, kinv_int)

    rhs = pl.pallas_call(
        rhs_kernel,
        out_shape=jax.ShapeDtypeStruct((3 * n_if, fourier), BF16),
        scratch_shapes=[pltpu.VMEM((3 * n_if, fourier), F32)],
        name="interface_rhs",
    )(load_if, part_a, got_a, part_b, got_b, analysis)

    peers = lax.axis_size("dom")
    me = lax.axis_index("dom").astype(jnp.int32)
    levels = peers.bit_length() - 1
    away = [j for j in range(peers) if j & 1]
    near = [j for j in range(peers) if not j & 1]
    sent = solve_blocks(me ^ jnp.asarray(away, jnp.int32), sinv, rhs, peers, F32)
    got = swapped(sent, "dom", 1)
    mine = solve_blocks(me ^ jnp.asarray(near, jnp.int32), sinv, rhs, peers, F32)
    for level in range(1, levels):
        both = (mine + got).reshape(peers >> (level + 1), 2, *mine.shape[1:])
        mine = both[:, 0]
        got = swapped(both[:, 1], "dom", 1 << level)
    rows = sinv.shape[0] // peers
    du_if = pl.pallas_call(
        last_kernel,
        out_shape=jax.ShapeDtypeStruct((rows // 3, width), F32),
        scratch_shapes=[pltpu.VMEM((rows, fourier), F32)],
        name="interface_result",
    )(mine, got)
    return (du_int, du_if, stress_end)


def solution(mesh):
    return jax.shard_map(
        per_device,
        mesh=mesh,
        in_specs=(
            P(("grp", "dom"), None),
            P("dom", None),
            P(("grp", "dom"), None),
            P("dom", None),
            P(("grp", "dom"), None),
            P(("grp", "dom"), None),
            P(("grp", "dom")),
            P(("grp", "dom")),
            P(("grp", "dom")),
            P(("grp", "dom")),
            P(("grp", "dom")),
            P(None, ("grp", "dom")),
            P(("grp", "dom"), None),
            P("grp", "dom"),
        ),
        out_specs=(P(("grp", "dom"), None), P(("grp", "dom"), None), P(None, ("grp", "dom"))),
        check_vma=False,
    )
```

```python
import functools
import math

import jax
import jax.numpy as jnp
import numpy as np
from jax import lax
from jax.experimental import pallas as pl
from jax.experimental.pallas import tpu as pltpu
from jax.sharding import PartitionSpec as P

TIMES = 32
POISSON = 0.3
LAME = POISSON / ((1.0 + POISSON) * (1.0 - 2.0 * POISSON))
SHEAR = 1.0 / (2.0 * (1.0 + POISSON))
HIGHEST = lax.Precision.HIGHEST
STEPS = 4
GROUPS = TIMES // STEPS
PART = 3 * STEPS
SLOT = 16
ROWS = GROUPS * SLOT
NT = (((1,), (1,)), ((), ()))
BF16 = jnp.bfloat16
F32 = jnp.float32


def strain_table():
    gauss = 1.0 / math.sqrt(3.0)
    table = np.zeros((6, 8, 8, 3))
    for point in range(8):
        coords = [((point >> bit & 1) * 2 - 1) * gauss for bit in range(3)]
        for corner in range(8):
            signs = [(corner >> bit & 1) * 2 - 1 for bit in range(3)]
            deriv = []
            for axis in range(3):
                value = signs[axis] / 8.0
                for other in range(3):
                    if other != axis:
                        value = value * (1.0 + signs[other] * coords[other])
                deriv.append(value)
            table[0, point, corner, 0] = deriv[0]
            table[1, point, corner, 1] = deriv[1]
            table[2, point, corner, 2] = deriv[2]
            table[3, point, corner, 0] = deriv[1]
            table[3, point, corner, 1] = deriv[0]
            table[4, point, corner, 1] = deriv[2]
            table[4, point, corner, 2] = deriv[1]
            table[5, point, corner, 2] = deriv[0]
            table[5, point, corner, 0] = deriv[2]
    return table.reshape(48, 24).astype(np.float32)


def time_tables(fourier):
    theta = 2.0 * math.pi * (np.arange(TIMES) + 0.3) / TIMES
    synthesis = np.zeros((fourier, TIMES))
    for column in range(fourier):
        harmonic = column // 2
        if column % 2 == 0:
            synthesis[column] = np.cos(harmonic * theta)
        else:
            synthesis[column] = np.sin((harmonic + 1) * theta)
    analysis = synthesis.T * (2.0 / TIMES)
    analysis[:, 0] = 1.0 / TIMES
    return synthesis.astype(np.float32), analysis.astype(np.float32)


def constants(fourier):
    synthesis, analysis = time_tables(fourier)
    differences = synthesis.astype(np.float64) - np.roll(synthesis.astype(np.float64), 1, axis=1)
    synth = np.zeros((GROUPS, 2, 3, STEPS, 3, fourier))
    anal = np.zeros((GROUPS, SLOT, 3, fourier))
    for comp in range(3):
        synth[:, :, comp, :, comp, :] = differences.T.reshape(GROUPS, 1, STEPS, fourier)
        anal[:, comp * STEPS : (comp + 1) * STEPS, comp, :] = analysis.reshape(GROUPS, STEPS, fourier)
    synth = jnp.asarray(synth.reshape(2 * GROUPS * PART, 3 * fourier), F32)
    table = strain_table().reshape(48, 8, 3)
    strain = np.zeros((STEPS, 48, 8, 2, 3, STEPS), np.float32)
    force = np.zeros((8, SLOT, STEPS, 48), np.float32)
    for step in range(STEPS):
        for half in range(2):
            strain[step, :, :, half, :, step] = table
        for comp in range(3):
            force[:, comp * STEPS + step, step, :] = table[:, :, comp].T
    high = synth.astype(BF16)
    low = (synth - high.astype(F32)).astype(BF16)
    return (
        high,
        low,
        jnp.asarray(strain.reshape(STEPS * 48, 16 * PART)).astype(BF16),
        jnp.asarray(force.reshape(8 * SLOT, STEPS * 48)).astype(BF16),
        jnp.asarray(anal.reshape(ROWS, 3 * fourier), F32),
    )


def up(n, to):
    return -(-n // to) * to


def element_kernel(*refs, neighbours, chunk, own, half):
    count_ref, int_ref, if_ref = refs[:3]
    halo_refs = refs[3 : 3 + neighbours]
    conn_ref, size_ref, stiff_ref, yield_ref, rate_ref, init_ref = refs[3 + neighbours : 9 + neighbours]
    high_ref, low_ref, strain_ref, force_ref = refs[9 + neighbours : 13 + neighbours]
    end_ref, pint_ref, pif_ref, back_ref = refs[13 + neighbours : 17 + neighbours]
    nodes, onehot, corners, forces, state, total = refs[17 + neighbours :]
    n_int, n_if, slots = int_ref.shape[1], if_ref.shape[1], halo_refs[0].shape[0]
    halo_at = up(own, 128)
    both = 2 * GROUPS * PART
    chunks = end_ref.shape[1] // chunk
    count = count_ref[0]
    used = lax.div(count + chunk - 1, chunk)

    nodes[...] = jnp.zeros_like(nodes)
    total[...] = jnp.zeros_like(total)
    halo = jnp.concatenate([ref[...].astype(F32) for ref in halo_refs], axis=0).astype(BF16)
    is_high = lax.rem(lax.broadcasted_iota(jnp.int32, (both, 1), 0), 2 * PART) < PART
    pieces = (
        (0, int_ref[...], (((1,), (0,)), ((), ()))),
        (n_int, if_ref[...], (((1,), (0,)), ((), ()))),
        (halo_at, halo, NT),
    )
    spans = []
    for start, rows, dims in pieces:
        value = lax.dot_general(high_ref[...], rows, dims, preferred_element_type=F32)
        value = value + lax.dot_general(low_ref[...], rows, dims, preferred_element_type=F32)
        upper = value.astype(BF16).astype(F32)
        value = jnp.where(is_high, upper, value - upper).astype(BF16)
        length = value.shape[1]
        cut = min(max(half - start, 0), length)
        if cut:
            nodes[:both, start : start + cut] = value[:, :cut]
        if cut < length:
            at = start + cut - half
            nodes[both:, at : at + length - cut] = value[:, cut:]

    def columns(c):
        return pl.ds(pl.multiple_of(c * chunk, chunk), chunk)

    def place(c, corner):
        node = conn_ref[pl.ds(corner, 1), columns(c)]
        node = node + jnp.where(node >= own, halo_at - own, 0)
        upper = node >= half
        return upper, node - jnp.where(upper, half, 0)

    def gather(c, corner):
        upper, node = place(c, corner)
        hot = jnp.where(lax.broadcasted_iota(jnp.int32, (half, chunk), 0) == node, 1.0, 0.0).astype(BF16)
        onehot[lax.rem(c, 3), corner] = hot
        found = jnp.dot(nodes[...], hot, preferred_element_type=F32)
        found = jnp.where(upper, found[both:], found[:both])
        rows = pl.ds(pl.multiple_of(corner * 2 * PART, 8), 2 * PART)
        for group in range(GROUPS):
            corners[lax.rem(c, 2), group, rows, :] = found[group * 2 * PART : (group + 1) * 2 * PART]

    def alive(c):
        slot = c * chunk + lax.broadcasted_iota(jnp.int32, (1, chunk), 1)
        return jnp.where(slot < count, 1.0, 0.0)

    def advance(c, group):
        at = columns(c)
        size, limit, rate = size_ref[:, at], yield_ref[:, at], rate_ref[:, at]
        modulus = stiff_ref[:, at] * (2.0 / size)

        def wide(row):
            return jnp.broadcast_to(row, (8, chunk))

        twice_shear, shear, lame = wide(modulus * (2.0 * SHEAR)), wide(modulus * SHEAR), wide(modulus * LAME)
        inverse, relax = wide(1.0 / limit), wide(rate * limit)
        scale = size * size * 0.25 * alive(c)
        corner_values = corners[lax.rem(c, 2), group].astype(BF16)
        delta = jnp.dot(strain_ref[...], corner_values, preferred_element_type=F32)
        stress = tuple(state[comp * 8 : comp * 8 + 8, :] for comp in range(6))
        history = []
        for step in range(STEPS):
            d = [delta[step * 48 + comp * 8 : step * 48 + comp * 8 + 8] for comp in range(6)]
            trace = lame * (d[0] + d[1] + d[2])
            stress = tuple(
                s + (twice_shear * d[comp] + trace if comp < 3 else shear * d[comp]) - relax * jnp.tanh(s * inverse)
                for comp, s in enumerate(stress)
            )
            history += list(stress)
        for comp in range(6):
            state[comp * 8 : comp * 8 + 8, :] = stress[comp]
        force = jnp.dot(force_ref[...], jnp.concatenate(history, axis=0).astype(BF16), preferred_element_type=F32)
        force = (force * scale).astype(BF16)
        rows = pl.ds(pl.multiple_of(group * SLOT, SLOT), SLOT)
        for corner in range(8):
            forces[lax.rem(c, 2), corner, rows, :] = force[corner * SLOT : (corner + 1) * SLOT]

    def scatter(c, corner):
        upper, _ = place(c, corner)
        part = forces[lax.rem(c, 2), corner].astype(F32)
        part = jnp.concatenate([jnp.where(upper, 0.0, part), jnp.where(upper, part, 0.0)], axis=0).astype(BF16)
        total[...] += lax.dot_general(onehot[lax.rem(c, 3), corner], part, NT, preferred_element_type=F32)

    turns = 4

    def stage(c, first, middle, last):
        if middle:
            state[...] = init_ref[:, columns(c)]

        @pl.loop(0, 8, step=turns)
        def _(turn):
            for k in range(turns) if last else ():
                scatter(c - 1, turn + k)
            for k in range(turns) if middle else ():
                advance(c, turn + k)
            for k in range(turns) if first else ():
                gather(c + 1, turn + k)

        if middle:
            end_ref[:, columns(c)] = state[...] * alive(c)

    stage(-1, True, False, False)

    @pl.when(used > 1)
    def _():
        stage(0, True, True, False)

        @pl.loop(1, used - 1)
        def _(c):
            stage(c, True, True, True)

        stage(used - 1, False, True, True)

    @pl.when(used == 1)
    def _():
        stage(0, False, True, False)

    stage(used, False, False, True)

    @pl.loop(used, chunks)
    def _(c):
        end_ref[:, columns(c)] = jnp.zeros((end_ref.shape[0], chunk), F32)

    def result(start, length):
        cut = min(max(half - start, 0), length)
        runs = []
        if cut:
            runs.append(total[start : start + cut, :ROWS])
        if cut < length:
            runs.append(total[start + cut - half : start + length - half, ROWS:])
        return runs[0] if len(runs) == 1 else jnp.concatenate(runs, axis=0)

    pint_ref[...] = result(0, n_int)
    pif_ref[...] = result(n_int, n_if)
    for slot_index in range(neighbours):
        back_ref[slot_index] = result(halo_at + slot_index * slots, slots)


def whole(shape):
    return pl.BlockSpec(shape, lambda *_: (0,) * len(shape))


def element_phase(count, u_int, u_if, halos, conn, params, stress_init, tables, interpret=False):
    chunk = 256
    n_int, n_if = u_int.shape[1], u_if.shape[1]
    own = n_int + n_if
    neighbours, slots = len(halos), halos[0].shape[0]
    half = up(up(own, 128) + neighbours * slots, 256) // 2
    half = up(half, 128)
    vmem = pl.BlockSpec(memory_space=pltpu.VMEM)
    inputs = [u_int, u_if, *halos, conn, *params, stress_init, *tables[:4]]
    return pl.pallas_call(
        functools.partial(element_kernel, neighbours=neighbours, chunk=chunk, own=own, half=half),
        in_specs=[pl.BlockSpec(memory_space=pltpu.SMEM)] + [vmem] * len(inputs),
        out_specs=[vmem] * 4,
        scratch_shapes=[
            pltpu.VMEM((4 * GROUPS * PART, half), BF16),
            pltpu.VMEM((3, 8, half, chunk), BF16),
            pltpu.VMEM((2, GROUPS, 16 * PART, chunk), F32),
            pltpu.VMEM((2, 8, ROWS, chunk), BF16),
            pltpu.VMEM((stress_init.shape[0], chunk), F32),
            pltpu.VMEM((half, 2 * ROWS), F32),
        ],
        out_shape=[
            jax.ShapeDtypeStruct(stress_init.shape, F32),
            jax.ShapeDtypeStruct((n_int, ROWS), F32),
            jax.ShapeDtypeStruct((n_if, ROWS), F32),
            jax.ShapeDtypeStruct((neighbours, slots, ROWS), F32),
        ],
        compiler_params=pltpu.CompilerParams(vmem_limit_bytes=60 << 20),
        name="elements",
        interpret=interpret,
    )(count, *inputs)


def send_kernel(int_ref, if_ref, map_ref, *out_refs):
    n_int, n_if = int_ref.shape[1], if_ref.shape[1]
    slots = map_ref.shape[1]
    for slot_index, out_ref in enumerate(out_refs):
        wanted = map_ref[slot_index : slot_index + 1, :]
        rows = None
        for first, ref in ((0, int_ref), (n_int, if_ref)):
            hot = lax.broadcasted_iota(jnp.int32, (ref.shape[1], slots), 0) + first == wanted
            hot = jnp.where(hot, 1.0, 0.0).astype(BF16)
            found = jnp.dot(ref[...], hot, preferred_element_type=F32)
            rows = found if rows is None else rows + found
        out_ref[...] = rows.T.astype(BF16)


def send_blocks(u_int, u_if, send_map):
    neighbours, slots = send_map.shape
    return pl.pallas_call(
        send_kernel,
        out_shape=[jax.ShapeDtypeStruct((slots, u_int.shape[0]), BF16)] * neighbours,
        name="halo_rows",
    )(u_int, u_if, send_map)


def added_back(own, map_ref, returned, first):
    for slot_index, ref in enumerate(returned):
        hot = (
            lax.broadcasted_iota(jnp.int32, (own.shape[0], ref.shape[0]), 0) + first
            == map_ref[slot_index : slot_index + 1, :]
        )
        hot = jnp.where(hot, 1.0, 0.0).astype(BF16)
        value = ref[...]
        high = value.astype(BF16)
        low = (value - high.astype(F32)).astype(BF16)
        own = own + jnp.dot(hot, high, preferred_element_type=F32) + jnp.dot(hot, low, preferred_element_type=F32)
    return own


def interface_kernel(own_ref, map_ref, *refs, first):
    returned, (a_ref, b_ref) = refs[:-2], refs[-2:]
    value = added_back(own_ref[...], map_ref, returned, first)
    half = a_ref.shape[0]
    a_ref[...] = value[:half]
    b_ref[...] = value[half:]


def interleaved(value, scratch):
    nodes, width = value.shape
    fourier = width // 3
    for comp in range(3):
        scratch[pl.ds(comp, nodes, stride=3), :] = value[:, comp * fourier : (comp + 1) * fourier]
    return scratch[...]


def separated(value, scratch):
    scratch[...] = value
    nodes = value.shape[0] // 3
    return jnp.concatenate([scratch[pl.ds(comp, nodes, stride=3), :] for comp in range(3)], axis=1)


def interior_kernel(own_ref, map_ref, *refs):
    returned = refs[:-5]
    load_ref, anal_ref, kinv_ref, du_ref, scratch = refs[-5:]
    value = added_back(own_ref[...], map_ref, returned, 0)
    force = jnp.dot(value, anal_ref[...], precision=HIGHEST, preferred_element_type=F32)
    rhs = interleaved(load_ref[...].T - force, scratch).astype(BF16)
    du = jnp.dot(kinv_ref[...], rhs, preferred_element_type=F32)
    du_ref[...] = separated(du, scratch).T


def solve_kernel(me_ref, load_ref, own_a, got_a, own_b, got_b, anal_ref, sinv_ref, *refs, peers):
    away_ref, near_ref, rhs, scratch, total, rows = refs
    index = pl.program_id(0)

    @pl.when(index == 0)
    def _():
        value = jnp.concatenate([own_a[...] + got_a[...], own_b[...] + got_b[...]], axis=0)
        force = jnp.dot(value, anal_ref[...], precision=HIGHEST, preferred_element_type=F32)
        right = interleaved(load_ref[...].T - force, scratch).T.astype(BF16)
        depth = rhs.shape[2]
        for block in range(rhs.shape[0]):
            rhs[block] = right[:, block * depth : (block + 1) * depth]

    term = jnp.dot(rhs[index], sinv_ref[...], preferred_element_type=F32)

    @pl.when(index == 0)
    def _():
        total[...] = term

    @pl.when(index > 0)
    def _():
        total[...] += term

    @pl.when(index == pl.num_programs(0) - 1)
    def _():
        rows[...] = total[...].T
        count = rows.shape[0] // peers
        for j in range(peers):
            at = (me_ref[0] ^ j) * count
            upper, lower = rows[pl.ds(at, count // 2), :], rows[pl.ds(at + count // 2, count // 2), :]
            out_ref = away_ref if j & 1 else near_ref
            out_ref[j // 2] = jnp.concatenate([upper, lower], axis=1).astype(out_ref.dtype)


def interface_solve(me, load, own_a, got_a, own_b, got_b, analysis, sinv, peers, dtype):
    depth_all, rows = sinv.shape
    blocks = next(b for b in (4, 3, 2, 1) if b == 1 or depth_all % (b * 16) == 0)
    depth = depth_all // blocks
    fourier = load.shape[0] // 3
    shape = (peers // 2, rows // peers // 2, 2 * fourier)
    small = [load, own_a, got_a, own_b, got_b, analysis]
    return pl.pallas_call(
        functools.partial(solve_kernel, peers=peers),
        grid_spec=pltpu.PrefetchScalarGridSpec(
            num_scalar_prefetch=1,
            grid=(blocks,),
            in_specs=[whole(x.shape) for x in small] + [pl.BlockSpec((depth, rows), lambda k, me: (k, 0))],
            out_specs=[whole(shape)] * 2,
            scratch_shapes=[
                pltpu.VMEM((blocks, fourier, depth), BF16),
                pltpu.VMEM((depth_all, fourier), F32),
                pltpu.VMEM((fourier, rows), F32),
                pltpu.VMEM((rows, fourier), F32),
            ],
        ),
        out_shape=[jax.ShapeDtypeStruct(shape, dtype), jax.ShapeDtypeStruct(shape, F32)],
        compiler_params=pltpu.CompilerParams(vmem_limit_bytes=40 << 20),
        name="interface_solve",
    )(me, *small, sinv)


def last_kernel(mine_ref, got_ref, out_ref, scratch):
    value = mine_ref[0] + got_ref[0].astype(F32)
    half = value.shape[0]
    fourier = value.shape[1] // 2
    out_ref[...] = separated(jnp.concatenate([value[:, :fourier], value[:, fourier:]], axis=0), scratch)


def swapped(shard, axis, bit):
    peers = lax.axis_size(axis)
    return lax.ppermute(shard, axis, [(i, i ^ bit) for i in range(peers)])


def passed_along(shard, axis, by):
    peers = lax.axis_size(axis)
    return lax.ppermute(shard, axis, [(i, (i + by) % peers) for i in range(peers)])


def per_device(
    u_int,
    u_if,
    load_int,
    load_if,
    conn,
    send_map,
    counts,
    elem_size,
    stiffness,
    yield_stress,
    relax_rate,
    stress_init,
    kinv_int,
    sinv,
):
    width = u_int.shape[1]
    fourier = width // 3
    n_int, n_if = u_int.shape[0], u_if.shape[0]
    neighbours, slots = send_map.shape
    reach = neighbours // 2
    offsets = list(range(-reach, 0)) + list(range(1, reach + 1))
    tables = constants(fourier)
    analysis = tables[4]

    blocks = send_blocks(u_int.T, u_if.T, send_map)
    halos = [passed_along(blocks[j], "dom", offsets[j]) for j in range(neighbours)]
    params = [x.reshape(1, -1) for x in (elem_size, stiffness, yield_stress, relax_rate)]
    stress_end, p_int, p_if, back = element_phase(
        counts, u_int.T, u_if.T, halos, conn.T, params, stress_init, tables
    )
    returned = [passed_along(back[j], "dom", -offsets[j]) for j in range(neighbours)]

    half = n_if // 2
    part_a, part_b = pl.pallas_call(
        functools.partial(interface_kernel, first=n_int),
        out_shape=[jax.ShapeDtypeStruct((half, ROWS), F32), jax.ShapeDtypeStruct((n_if - half, ROWS), F32)],
        name="interface_forces",
    )(p_if, send_map, *returned)

    bits = [1 << b for b in range(lax.axis_size("grp").bit_length() - 1)]
    got_a = got_b = None
    for bit_a, bit_b in zip(bits, bits[::-1]):
        if got_a is not None:
            part_a, part_b = part_a + got_a, part_b + got_b
        got_a, got_b = swapped(part_a, "grp", bit_a), swapped(part_b, "grp", bit_b)

    du_int = pl.pallas_call(
        interior_kernel,
        out_shape=jax.ShapeDtypeStruct((width, n_int), F32),
        scratch_shapes=[pltpu.VMEM((3 * n_int, fourier), F32)],
        cost_estimate=pl.CostEstimate(
            flops=2 * kinv_int.size * fourier, bytes_accessed=2 * kinv_int.size, transcendentals=0
        ),
        name="interior_solve",
    )(p_int, send_map, *returned, load_int.T, analysis, kinv_int).T

    peers = lax.axis_size("dom")
    me = lax.axis_index("dom").astype(jnp.int32).reshape(1)
    levels = peers.bit_length() - 1
    sent, mine = interface_solve(
        me, load_if.T, part_a, got_a, part_b, got_b, analysis, sinv.T, peers, F32
    )
    got = swapped(sent, "dom", 1)
    for level in range(1, levels):
        both = (mine + got).reshape(peers >> (level + 1), 2, *mine.shape[1:])
        mine = both[:, 0]
        got = swapped(both[:, 1], "dom", 1 << level)
    rows = sinv.shape[0] // peers
    du_if = pl.pallas_call(
        last_kernel,
        out_shape=jax.ShapeDtypeStruct((rows // 3, width), F32),
        scratch_shapes=[pltpu.VMEM((rows, fourier), F32)],
        name="interface_result",
    )(mine, got)
    return (du_int, du_if, stress_end)


def solution(mesh):
    return jax.shard_map(
        per_device,
        mesh=mesh,
        in_specs=(
            P(("grp", "dom"), None),
            P("dom", None),
            P(("grp", "dom"), None),
            P("dom", None),
            P(("grp", "dom"), None),
            P(("grp", "dom"), None),
            P(("grp", "dom")),
            P(("grp", "dom")),
            P(("grp", "dom")),
            P(("grp", "dom")),
            P(("grp", "dom")),
            P(None, ("grp", "dom")),
            P(("grp", "dom"), None),
            P("grp", "dom"),
        ),
        out_specs=(P(("grp", "dom"), None), P(("grp", "dom"), None), P(None, ("grp", "dom"))),
        check_vma=False,
    )
```

```python
import functools
import math

import jax
import jax.numpy as jnp
import numpy as np
from jax import lax
from jax.experimental import pallas as pl
from jax.experimental.pallas import tpu as pltpu
from jax.sharding import PartitionSpec as P

TIMES = 32
POISSON = 0.3
LAME = POISSON / ((1.0 + POISSON) * (1.0 - 2.0 * POISSON))
SHEAR = 1.0 / (2.0 * (1.0 + POISSON))
HIGHEST = lax.Precision.HIGHEST
STEPS = 4
GROUPS = TIMES // STEPS
PART = 3 * STEPS
SLOT = 16
ROWS = GROUPS * SLOT
NT = (((1,), (1,)), ((), ()))


def lasts(microseconds):
    return pl.CostEstimate(flops=0, bytes_accessed=int(3e6 * microseconds), transcendentals=0)


LIMIT = 38
SMALL = pltpu.CompilerParams(vmem_limit_bytes=12 << 20)
BF16 = jnp.bfloat16
F32 = jnp.float32


def strain_table():
    gauss = 1.0 / math.sqrt(3.0)
    table = np.zeros((6, 8, 8, 3))
    for point in range(8):
        coords = [((point >> bit & 1) * 2 - 1) * gauss for bit in range(3)]
        for corner in range(8):
            signs = [(corner >> bit & 1) * 2 - 1 for bit in range(3)]
            deriv = []
            for axis in range(3):
                value = signs[axis] / 8.0
                for other in range(3):
                    if other != axis:
                        value = value * (1.0 + signs[other] * coords[other])
                deriv.append(value)
            table[0, point, corner, 0] = deriv[0]
            table[1, point, corner, 1] = deriv[1]
            table[2, point, corner, 2] = deriv[2]
            table[3, point, corner, 0] = deriv[1]
            table[3, point, corner, 1] = deriv[0]
            table[4, point, corner, 1] = deriv[2]
            table[4, point, corner, 2] = deriv[1]
            table[5, point, corner, 2] = deriv[0]
            table[5, point, corner, 0] = deriv[2]
    return table.reshape(48, 24).astype(np.float32)


def time_tables(fourier):
    theta = 2.0 * math.pi * (np.arange(TIMES) + 0.3) / TIMES
    synthesis = np.zeros((fourier, TIMES))
    for column in range(fourier):
        harmonic = column // 2
        if column % 2 == 0:
            synthesis[column] = np.cos(harmonic * theta)
        else:
            synthesis[column] = np.sin((harmonic + 1) * theta)
    analysis = synthesis.T * (2.0 / TIMES)
    analysis[:, 0] = 1.0 / TIMES
    return synthesis.astype(np.float32), analysis.astype(np.float32)


def constants(fourier):
    synthesis, analysis = time_tables(fourier)
    differences = synthesis.astype(np.float64) - np.roll(synthesis.astype(np.float64), 1, axis=1)
    synth = np.zeros((GROUPS, 2, 3, STEPS, 3, fourier))
    anal = np.zeros((GROUPS, SLOT, 3, fourier))
    for comp in range(3):
        synth[:, :, comp, :, comp, :] = differences.T.reshape(GROUPS, 1, STEPS, fourier)
        anal[:, comp * STEPS : (comp + 1) * STEPS, comp, :] = analysis.reshape(GROUPS, STEPS, fourier)
    synth = jnp.asarray(synth.reshape(2 * GROUPS * PART, 3 * fourier), F32)
    table = strain_table().reshape(48, 8, 3)
    strain = np.zeros((STEPS, 48, 8, 2, 3, STEPS), np.float32)
    force = np.zeros((8, SLOT, STEPS, 48), np.float32)
    for step in range(STEPS):
        for half in range(2):
            strain[step, :, :, half, :, step] = table
        for comp in range(3):
            force[:, comp * STEPS + step, step, :] = table[:, :, comp].T
    high = synth.astype(BF16)
    low = (synth - high.astype(F32)).astype(BF16)
    return (
        high,
        low,
        jnp.asarray(strain.reshape(STEPS * 48, 16 * PART)).astype(BF16),
        jnp.asarray(force.reshape(8 * SLOT, STEPS * 48)).astype(BF16),
        jnp.asarray(anal.reshape(ROWS, 3 * fourier), F32),
    )


def up(n, to):
    return -(-n // to) * to


def element_kernel(*refs, neighbours, chunk, own, half, kept):
    refs = list(refs)

    def take(n):
        taken, refs[:n] = refs[:n], []
        return taken

    count_ref, int_ref, if_ref = take(3)
    halo_refs = take(neighbours)
    conn_ref, size_ref, stiff_ref, yield_ref, rate_ref, init_ref = take(6)
    high_ref, low_ref, strain_ref, force_ref = take(4)
    far_refs = take(kept)
    end_ref, pint_ref, pif_ref = take(3)
    back_refs = take(neighbours)
    near_refs = take(kept)
    nodes, onehot, corners, forces, state, total, arrived = refs
    fetches = [
        pltpu.make_async_copy(far, near, arrived.at[k]) for k, (far, near) in enumerate(zip(far_refs, near_refs))
    ]
    for fetch in fetches:
        fetch.start()
    n_int, n_if, slots = int_ref.shape[1], if_ref.shape[1], halo_refs[0].shape[0]
    halo_at = up(own, 128)
    both = 2 * GROUPS * PART
    chunks = end_ref.shape[1] // chunk
    count = count_ref[0]
    used = jnp.maximum(lax.div(count + chunk - 1, chunk), 1)

    nodes[...] = jnp.zeros_like(nodes)
    total[...] = jnp.zeros_like(total)
    halo = jnp.concatenate([ref[...].astype(F32) for ref in halo_refs], axis=0).astype(BF16)
    is_high = lax.rem(lax.broadcasted_iota(jnp.int32, (both, 1), 0), 2 * PART) < PART
    pieces = (
        (0, int_ref[...], (((1,), (0,)), ((), ()))),
        (n_int, if_ref[...], (((1,), (0,)), ((), ()))),
        (halo_at, halo, NT),
    )
    spans = []
    for start, rows, dims in pieces:
        value = lax.dot_general(high_ref[...], rows, dims, preferred_element_type=F32)
        value = value + lax.dot_general(low_ref[...], rows, dims, preferred_element_type=F32)
        upper = value.astype(BF16).astype(F32)
        value = jnp.where(is_high, upper, value - upper).astype(BF16)
        length = value.shape[1]
        cut = min(max(half - start, 0), length)
        if cut:
            nodes[:both, start : start + cut] = value[:, :cut]
        if cut < length:
            at = start + cut - half
            nodes[both:, at : at + length - cut] = value[:, cut:]

    def columns(c):
        return pl.ds(pl.multiple_of(c * chunk, chunk), chunk)

    def place(c, corner):
        node = conn_ref[pl.ds(corner, 1), columns(c)]
        node = node + jnp.where(node >= own, halo_at - own, 0)
        upper = node >= half
        return upper, node - jnp.where(upper, half, 0)

    def gather(c, corner):
        upper, node = place(c, corner)
        hot = jnp.where(lax.broadcasted_iota(jnp.int32, (half, chunk), 0) == node, 1.0, 0.0).astype(BF16)
        onehot[lax.rem(c, 3), corner] = hot
        found = jnp.dot(nodes[...], hot, preferred_element_type=F32)
        found = jnp.where(upper, found[both:], found[:both])
        rows = pl.ds(pl.multiple_of(corner * 2 * PART, 8), 2 * PART)
        for group in range(GROUPS):
            corners[lax.rem(c, 2), group, rows, :] = found[group * 2 * PART : (group + 1) * 2 * PART]

    def alive(c):
        slot = c * chunk + lax.broadcasted_iota(jnp.int32, (1, chunk), 1)
        return jnp.where(slot < count, 1.0, 0.0)

    def advance(c, group):
        at = columns(c)
        size, limit, rate = size_ref[:, at], yield_ref[:, at], rate_ref[:, at]
        modulus = stiff_ref[:, at] * (2.0 / size)

        def wide(row):
            return jnp.broadcast_to(row, (8, chunk))

        twice_shear, shear, lame = wide(modulus * (2.0 * SHEAR)), wide(modulus * SHEAR), wide(modulus * LAME)
        inverse, relax = wide(1.0 / limit), wide(rate * limit)
        scale = size * size * 0.25 * alive(c)
        corner_values = corners[lax.rem(c, 2), group].astype(BF16)
        delta = jnp.dot(strain_ref[...], corner_values, preferred_element_type=F32)
        stress = tuple(state[comp * 8 : comp * 8 + 8, :] for comp in range(6))
        history = []
        for step in range(STEPS):
            d = [delta[step * 48 + comp * 8 : step * 48 + comp * 8 + 8] for comp in range(6)]
            trace = lame * (d[0] + d[1] + d[2])
            stress = tuple(
                s + (twice_shear * d[comp] + trace if comp < 3 else shear * d[comp]) - relax * jnp.tanh(s * inverse)
                for comp, s in enumerate(stress)
            )
            history += list(stress)
        for comp in range(6):
            state[comp * 8 : comp * 8 + 8, :] = stress[comp]
        force = jnp.dot(force_ref[...], jnp.concatenate(history, axis=0).astype(BF16), preferred_element_type=F32)
        force = (force * scale).astype(BF16)
        rows = pl.ds(pl.multiple_of(group * SLOT, SLOT), SLOT)
        for corner in range(8):
            forces[lax.rem(c, 2), corner, rows, :] = force[corner * SLOT : (corner + 1) * SLOT]

    def scatter(c, corner):
        upper, _ = place(c, corner)
        part = forces[lax.rem(c, 2), corner].astype(F32)
        part = jnp.concatenate([jnp.where(upper, 0.0, part), jnp.where(upper, part, 0.0)], axis=0).astype(BF16)
        total[...] += lax.dot_general(onehot[lax.rem(c, 3), corner], part, NT, preferred_element_type=F32)

    turns = 4

    def stage(c, first, middle, last):
        if middle:
            state[...] = init_ref[:, columns(c)]

        @pl.loop(0, 8, step=turns)
        def _(turn):
            for k in range(turns) if last else ():
                scatter(c - 1, turn + k)
            for k in range(turns) if middle else ():
                advance(c, turn + k)
            for k in range(turns) if first else ():
                gather(c + 1, turn + k)

        if middle:
            end_ref[:, columns(c)] = state[...] * alive(c)

    stage(-1, True, False, False)

    @pl.when(used > 1)
    def _():
        stage(0, True, True, False)

        @pl.loop(1, used - 1)
        def _(c):
            stage(c, True, True, True)

        stage(used - 1, False, True, True)

    @pl.when(used == 1)
    def _():
        stage(0, False, True, False)

    stage(used, False, False, True)

    @pl.loop(used, chunks)
    def _(c):
        end_ref[:, columns(c)] = jnp.zeros((end_ref.shape[0], chunk), F32)

    def result(start, length):
        cut = min(max(half - start, 0), length)
        runs = []
        if cut:
            runs.append(total[start : start + cut, :ROWS])
        if cut < length:
            runs.append(total[start + cut - half : start + length - half, ROWS:])
        return runs[0] if len(runs) == 1 else jnp.concatenate(runs, axis=0)

    pint_ref[...] = result(0, n_int)
    pif_ref[...] = result(n_int, n_if)
    for slot_index, back_ref in enumerate(back_refs):
        back_ref[...] = result(halo_at + slot_index * slots, slots)
    for fetch in fetches:
        fetch.wait()


def whole(shape):
    return pl.BlockSpec(shape, lambda *_: (0,) * len(shape))


def element_phase(count, u_int, u_if, halos, conn, params, stress_init, tables, later=(), interpret=False):
    chunk = 256
    n_int, n_if = u_int.shape[1], u_if.shape[1]
    own = n_int + n_if
    neighbours, slots = len(halos), halos[0].shape[0]
    half = up(up(own, 128) + neighbours * slots, 256) // 2
    half = up(half, 128)
    vmem = pl.BlockSpec(memory_space=pltpu.VMEM)
    inputs = [u_int, u_if, *halos, conn, *params, stress_init, *tables[:4]]
    return pl.pallas_call(
        functools.partial(element_kernel, neighbours=neighbours, chunk=chunk, own=own, half=half, kept=len(later)),
        in_specs=[pl.BlockSpec(memory_space=pltpu.SMEM)] + [vmem] * len(inputs)
        + [pl.BlockSpec(memory_space=pl.ANY)] * len(later),
        out_specs=[vmem] * (3 + neighbours + len(later)),
        scratch_shapes=[
            pltpu.VMEM((4 * GROUPS * PART, half), BF16),
            pltpu.VMEM((3, 8, half, chunk), BF16),
            pltpu.VMEM((2, GROUPS, 16 * PART, chunk), F32),
            pltpu.VMEM((2, 8, ROWS, chunk), BF16),
            pltpu.VMEM((stress_init.shape[0], chunk), F32),
            pltpu.VMEM((half, 2 * ROWS), F32),
            pltpu.SemaphoreType.DMA((max(len(later), 1),)),
        ],
        out_shape=[
            jax.ShapeDtypeStruct(stress_init.shape, F32),
            pltpu.VMEM((n_int, ROWS), F32),
            pltpu.VMEM((n_if, ROWS), F32),
        ]
        + [pltpu.VMEM((slots, ROWS), F32)] * neighbours
        + [pltpu.VMEM(x.shape, x.dtype) for x in later],
        compiler_params=pltpu.CompilerParams(vmem_limit_bytes=LIMIT << 20),
        cost_estimate=lasts(40),
        name="elements",
        interpret=interpret,
    )(count, *inputs, *later)


def send_kernel(int_ref, if_ref, map_ref, *out_refs):
    n_int, n_if = int_ref.shape[1], if_ref.shape[1]
    slots = map_ref.shape[1]
    for slot_index, out_ref in enumerate(out_refs):
        wanted = map_ref[slot_index : slot_index + 1, :]
        rows = None
        for first, ref in ((0, int_ref), (n_int, if_ref)):
            hot = lax.broadcasted_iota(jnp.int32, (ref.shape[1], slots), 0) + first == wanted
            hot = jnp.where(hot, 1.0, 0.0).astype(BF16)
            found = jnp.dot(ref[...], hot, preferred_element_type=F32)
            rows = found if rows is None else rows + found
        out_ref[...] = rows.T.astype(BF16)


def send_blocks(u_int, u_if, send_map):
    neighbours, slots = send_map.shape
    return pl.pallas_call(
        send_kernel,
        out_shape=[jax.ShapeDtypeStruct((slots, u_int.shape[0]), BF16)] * neighbours,
        compiler_params=pltpu.CompilerParams(vmem_limit_bytes=60 << 20), cost_estimate=lasts(3), name="halo_rows",
    )(u_int, u_if, send_map)


def added_back(own, map_ref, returned, first):
    for slot_index, ref in enumerate(returned):
        hot = (
            lax.broadcasted_iota(jnp.int32, (own.shape[0], ref.shape[0]), 0) + first
            == map_ref[slot_index : slot_index + 1, :]
        )
        hot = jnp.where(hot, 1.0, 0.0).astype(BF16)
        value = ref[...]
        high = value.astype(BF16)
        low = (value - high.astype(F32)).astype(BF16)
        own = own + jnp.dot(hot, high, preferred_element_type=F32) + jnp.dot(hot, low, preferred_element_type=F32)
    return own


def interface_kernel(own_ref, map_ref, *refs, first):
    returned, outs = refs[:-4], refs[-4:]
    value = added_back(own_ref[...], map_ref, returned, first)
    half = outs[0].shape[0]
    for part, rows in enumerate((value[:half], value[half:])):
        outs[part][...] = rows
        outs[2 + part][...] = rows.astype(BF16)


def join_kernel(own_a, got_a, own_b, got_b, a_ref, b_ref, sent_a, sent_b):
    for own, got, ref, sent in ((own_a, got_a, a_ref, sent_a), (own_b, got_b, b_ref, sent_b)):
        value = own[...] + got[...].astype(F32)
        ref[...] = value
        sent[...] = value.astype(BF16)


def halves(n_rows):
    sizes = (n_rows // 2, n_rows - n_rows // 2)
    return [jax.ShapeDtypeStruct((size, ROWS), kind) for kind in (F32, BF16) for size in sizes]


def interleaved(value, scratch):
    nodes, width = value.shape
    fourier = width // 3
    for comp in range(3):
        scratch[pl.ds(comp, nodes, stride=3), :] = value[:, comp * fourier : (comp + 1) * fourier]
    return scratch[...]


def separated(value, scratch):
    scratch[...] = value
    nodes = value.shape[0] // 3
    return jnp.concatenate([scratch[pl.ds(comp, nodes, stride=3), :] for comp in range(3)], axis=1)


def interior_rhs_kernel(own_ref, map_ref, *refs):
    returned = refs[:-4]
    load_ref, anal_ref, rhs_ref, scratch = refs[-4:]
    value = added_back(own_ref[...], map_ref, returned, 0)
    force = jnp.dot(value, anal_ref[...], precision=HIGHEST, preferred_element_type=F32)
    rhs_ref[...] = interleaved(load_ref[...].T - force, scratch).astype(BF16)


def interior_kernel(rhs_ref, kinv_ref, du_ref, scratch):
    du = jnp.dot(kinv_ref[...], rhs_ref[...], preferred_element_type=F32)
    du_ref[...] = separated(du, scratch).T


def solve_kernel(load_ref, own_a, got_a, own_b, got_b, anal_ref, sinv_ref, *refs, peers):
    away_ref, near_ref, scratch, total, rows = refs
    depth_all = sinv_ref.shape[0]
    blocks = next(b for b in (4, 3, 2, 1) if b == 1 or depth_all % (b * 16) == 0)
    depth = depth_all // blocks
    value = jnp.concatenate([own_a[...] + got_a[...].astype(F32), own_b[...] + got_b[...].astype(F32)], axis=0)
    force = jnp.dot(value, anal_ref[...], precision=HIGHEST, preferred_element_type=F32)
    right = interleaved(load_ref[...].T - force, scratch).T.astype(BF16)
    for k in range(blocks):
        part = slice(k * depth, (k + 1) * depth)
        term = jnp.dot(right[:, part], sinv_ref[part, :], preferred_element_type=F32)
        total[...] = term if k == 0 else total[...] + term
    rows[...] = total[...].T
    count = rows.shape[0] // peers
    me = lax.axis_index("dom")
    for j in range(peers):
        at = (me ^ j) * count
        upper, lower = rows[pl.ds(at, count // 2), :], rows[pl.ds(at + count // 2, count // 2), :]
        out_ref = away_ref if j & 1 else near_ref
        out_ref[j // 2] = jnp.concatenate([upper, lower], axis=1).astype(out_ref.dtype)


def interface_solve(load, own_a, got_a, own_b, got_b, analysis, sinv, peers):
    depth, rows = sinv.shape
    fourier = load.shape[0] // 3
    shape = (peers // 2, rows // peers // 2, 2 * fourier)
    vmem = pl.BlockSpec(memory_space=pltpu.VMEM)
    small = [load, own_a, got_a, own_b, got_b, analysis]
    return pl.pallas_call(
        functools.partial(solve_kernel, peers=peers),
        in_specs=[vmem] * (len(small) + 1),
        out_specs=[vmem] * 2,
        scratch_shapes=[
            pltpu.VMEM((depth, fourier), F32),
            pltpu.VMEM((fourier, rows), F32),
            pltpu.VMEM((rows, fourier), F32),
        ],
        out_shape=[jax.ShapeDtypeStruct(shape, BF16), jax.ShapeDtypeStruct(shape, F32)],
        compiler_params=pltpu.CompilerParams(vmem_limit_bytes=12 << 20),
        cost_estimate=lasts(10),
        name="interface_solve",
    )(*small, sinv)


def split_kernel(mine_ref, got_ref, *outs):
    keep_ref, sent = outs[0], outs[1:]
    for j in range(mine_ref.shape[0]):
        value = mine_ref[j] + got_ref[j].astype(F32)
        if len(sent) == 1:
            ref = sent[0] if j & 1 else keep_ref
            ref[j // 2] = value.astype(ref.dtype)
        elif j == 0:
            keep_ref[...] = value
        else:
            sent[j - 1][...] = value.astype(BF16)


def split(mine, got, apart):
    count, shape = mine.shape[0], mine.shape[1:]
    if apart:
        outs = [jax.ShapeDtypeStruct(shape, F32)] + [jax.ShapeDtypeStruct(shape, BF16)] * (count - 1)
    else:
        outs = [jax.ShapeDtypeStruct((count // 2, *shape), kind) for kind in (F32, BF16)]
    return pl.pallas_call(split_kernel, out_shape=outs, compiler_params=SMALL, cost_estimate=lasts(4), name="correction_sums")(mine, got)


def last_kernel(mine_ref, *refs):
    got_refs, (out_ref, scratch) = refs[:-2], refs[-2:]
    value = mine_ref[...]
    for ref in got_refs:
        value = value + ref[...].astype(F32)
    fourier = value.shape[1] // 2
    out_ref[...] = separated(jnp.concatenate([value[:, :fourier], value[:, fourier:]], axis=0), scratch)


def swapped(shard, axis, bit):
    peers = lax.axis_size(axis)
    return lax.ppermute(shard, axis, [(i, i ^ bit) for i in range(peers)])


def passed_along(shard, axis, by):
    peers = lax.axis_size(axis)
    return lax.ppermute(shard, axis, [(i, (i + by) % peers) for i in range(peers)])


def per_device(
    u_int,
    u_if,
    load_int,
    load_if,
    conn,
    send_map,
    counts,
    elem_size,
    stiffness,
    yield_stress,
    relax_rate,
    stress_init,
    kinv_int,
    sinv,
):
    width = u_int.shape[1]
    fourier = width // 3
    n_int, n_if = u_int.shape[0], u_if.shape[0]
    neighbours, slots = send_map.shape
    reach = neighbours // 2
    offsets = list(range(-reach, 0)) + list(range(1, reach + 1))
    tables = constants(fourier)
    analysis = tables[4]

    blocks = send_blocks(u_int.T, u_if.T, send_map)
    halos = [passed_along(blocks[j], "dom", offsets[j]) for j in range(neighbours)]
    params = [x.reshape(1, -1) for x in (elem_size, stiffness, yield_stress, relax_rate)]
    later = (sinv.T, kinv_int, load_int.T, load_if.T, analysis, send_map)
    stress_end, p_int, p_if, *more = element_phase(
        counts, u_int.T, u_if.T, halos, conn.T, params, stress_init, tables, later
    )
    back = more[:neighbours]
    sinv_t, kinv, load_int_t, load_if_t, analysis, near_map = (
        pltpu.with_memory_space_constraint(x, pltpu.VMEM) for x in more[neighbours:]
    )
    returned = [passed_along(back[j], "dom", -offsets[j]) for j in range(neighbours)]

    part_a, part_b, sent_a, sent_b = pl.pallas_call(
        functools.partial(interface_kernel, first=n_int), out_shape=halves(n_if), compiler_params=SMALL, cost_estimate=lasts(4), name="interface_forces"
    )(p_if, near_map, *returned)

    rhs_int = pl.pallas_call(
        interior_rhs_kernel,
        out_shape=jax.ShapeDtypeStruct((3 * n_int, fourier), BF16),
        scratch_shapes=[pltpu.VMEM((3 * n_int, fourier), F32)],
        compiler_params=SMALL, cost_estimate=lasts(12), name="interior_rhs",
    )(p_int, near_map, *returned, load_int_t, analysis)

    bits = [1 << b for b in range(lax.axis_size("grp").bit_length() - 1)]
    for turn, (bit_a, bit_b) in enumerate(zip(bits, bits[::-1])):
        if turn:
            part_a, part_b, sent_a, sent_b = pl.pallas_call(
                join_kernel, out_shape=halves(n_if), compiler_params=SMALL, cost_estimate=lasts(5), name="interface_sums"
            )(part_a, got_a, part_b, got_b)
            sent_a, sent_b, rhs_int = lax.optimization_barrier((sent_a, sent_b, rhs_int))
        got_a, got_b = swapped(sent_a, "grp", bit_a), swapped(sent_b, "grp", bit_b)

    du_int = pl.pallas_call(
        interior_kernel,
        out_shape=jax.ShapeDtypeStruct((width, n_int), F32),
        scratch_shapes=[pltpu.VMEM((3 * n_int, fourier), F32)],
        compiler_params=SMALL, cost_estimate=lasts(6), name="interior_solve",
    )(rhs_int, kinv).T

    peers = lax.axis_size("dom")
    sent, mine = interface_solve(load_if_t, part_a, got_a, part_b, got_b, analysis, sinv_t, peers)
    bit = 1
    while True:
        got = swapped(sent, "dom", bit)
        apart = mine.shape[0] <= 4
        mine, *sent = split(mine, got, apart)
        bit *= 2
        if apart:
            break
        sent = sent[0]
    got = [swapped(block, "dom", bit * (j + 1)) for j, block in enumerate(sent)]
    rows = sinv.shape[0] // peers
    du_if = pl.pallas_call(
        last_kernel,
        out_shape=jax.ShapeDtypeStruct((rows // 3, width), F32),
        scratch_shapes=[pltpu.VMEM((rows, fourier), F32)],
        compiler_params=SMALL, cost_estimate=lasts(2), name="interface_result",
    )(mine, *got)
    return (du_int, du_if, stress_end)


def solution(mesh):
    return jax.shard_map(
        per_device,
        mesh=mesh,
        in_specs=(
            P(("grp", "dom"), None),
            P("dom", None),
            P(("grp", "dom"), None),
            P("dom", None),
            P(("grp", "dom"), None),
            P(("grp", "dom"), None),
            P(("grp", "dom")),
            P(("grp", "dom")),
            P(("grp", "dom")),
            P(("grp", "dom")),
            P(("grp", "dom")),
            P(None, ("grp", "dom")),
            P(("grp", "dom"), None),
            P("grp", "dom"),
        ),
        out_specs=(P(("grp", "dom"), None), P(("grp", "dom"), None), P(None, ("grp", "dom"))),
        check_vma=False,
    )
```

```python
import functools
import math

import jax
import jax.numpy as jnp
import numpy as np
from jax import lax
from jax.experimental import pallas as pl
from jax.experimental.pallas import tpu as pltpu
from jax.sharding import PartitionSpec as P

TIMES = 32
POISSON = 0.3
LAME = POISSON / ((1.0 + POISSON) * (1.0 - 2.0 * POISSON))
SHEAR = 1.0 / (2.0 * (1.0 + POISSON))
HIGHEST = lax.Precision.HIGHEST
STEPS = 4
GROUPS = TIMES // STEPS
PART = 3 * STEPS
SLOT = 16
ROWS = GROUPS * SLOT
NT = (((1,), (1,)), ((), ()))


def lasts(microseconds):
    return pl.CostEstimate(flops=0, bytes_accessed=int(3e6 * microseconds), transcendentals=0)


LIMIT = 34
SMALL = pltpu.CompilerParams(vmem_limit_bytes=12 << 20)
BF16 = jnp.bfloat16
F32 = jnp.float32


def strain_table():
    gauss = 1.0 / math.sqrt(3.0)
    table = np.zeros((6, 8, 8, 3))
    for point in range(8):
        coords = [((point >> bit & 1) * 2 - 1) * gauss for bit in range(3)]
        for corner in range(8):
            signs = [(corner >> bit & 1) * 2 - 1 for bit in range(3)]
            deriv = []
            for axis in range(3):
                value = signs[axis] / 8.0
                for other in range(3):
                    if other != axis:
                        value = value * (1.0 + signs[other] * coords[other])
                deriv.append(value)
            table[0, point, corner, 0] = deriv[0]
            table[1, point, corner, 1] = deriv[1]
            table[2, point, corner, 2] = deriv[2]
            table[3, point, corner, 0] = deriv[1]
            table[3, point, corner, 1] = deriv[0]
            table[4, point, corner, 1] = deriv[2]
            table[4, point, corner, 2] = deriv[1]
            table[5, point, corner, 2] = deriv[0]
            table[5, point, corner, 0] = deriv[2]
    return table.reshape(48, 24).astype(np.float32)


def time_tables(fourier):
    theta = 2.0 * math.pi * (np.arange(TIMES) + 0.3) / TIMES
    synthesis = np.zeros((fourier, TIMES))
    for column in range(fourier):
        harmonic = column // 2
        if column % 2 == 0:
            synthesis[column] = np.cos(harmonic * theta)
        else:
            synthesis[column] = np.sin((harmonic + 1) * theta)
    analysis = synthesis.T * (2.0 / TIMES)
    analysis[:, 0] = 1.0 / TIMES
    return synthesis.astype(np.float32), analysis.astype(np.float32)


def constants(fourier):
    synthesis, analysis = time_tables(fourier)
    differences = synthesis.astype(np.float64) - np.roll(synthesis.astype(np.float64), 1, axis=1)
    synth = np.zeros((GROUPS, 2, 3, STEPS, 3, fourier))
    anal = np.zeros((GROUPS, SLOT, 3, fourier))
    for comp in range(3):
        synth[:, :, comp, :, comp, :] = differences.T.reshape(GROUPS, 1, STEPS, fourier)
        anal[:, comp * STEPS : (comp + 1) * STEPS, comp, :] = analysis.reshape(GROUPS, STEPS, fourier)
    synth = jnp.asarray(synth.reshape(2 * GROUPS * PART, 3 * fourier), F32)
    table = strain_table().reshape(48, 8, 3)
    strain = np.zeros((STEPS, 48, 8, 2, 3, STEPS), np.float32)
    force = np.zeros((8, SLOT, STEPS, 48), np.float32)
    for step in range(STEPS):
        for half in range(2):
            strain[step, :, :, half, :, step] = table
        for comp in range(3):
            force[:, comp * STEPS + step, step, :] = table[:, :, comp].T
    high = synth.astype(BF16)
    low = (synth - high.astype(F32)).astype(BF16)
    return (
        high,
        low,
        jnp.asarray(strain.reshape(STEPS * 48, 16 * PART)).astype(BF16),
        jnp.asarray(force.reshape(8 * SLOT, STEPS * 48)).astype(BF16),
        jnp.asarray(anal.reshape(ROWS, 3 * fourier), F32),
    )


def up(n, to):
    return -(-n // to) * to


def node_values(rows, dims, high_ref, low_ref):
    value = lax.dot_general(high_ref[...], rows, dims, preferred_element_type=F32)
    value = value + lax.dot_general(low_ref[...], rows, dims, preferred_element_type=F32)
    upper = value.astype(BF16).astype(F32)
    row = lax.broadcasted_iota(jnp.int32, (value.shape[0], 1), 0)
    return jnp.where(lax.rem(row, 2 * PART) < PART, upper, value - upper).astype(BF16)


def put_nodes(nodes, start, value):
    both, half, length = nodes.shape[0] // 2, nodes.shape[1], value.shape[1]
    cut = min(max(half - start, 0), length)
    if cut:
        nodes[:both, start : start + cut] = value[:, :cut]
    if cut < length:
        at = start + cut - half
        nodes[both:, at : at + length - cut] = value[:, cut:]


def prepare_kernel(int_ref, if_ref, *refs):
    kept = len(refs) // 2 - 1
    far_refs, nodes, near_refs, arrived = refs[:kept], refs[kept], refs[kept + 1 : -1], refs[-1]
    fetches = [
        pltpu.make_async_copy(far, near, arrived.at[k]) for k, (far, near) in enumerate(zip(far_refs, near_refs))
    ]
    for fetch in fetches:
        fetch.start()
    nodes[...] = jnp.zeros_like(nodes)
    for fetch in fetches[:2]:
        fetch.wait()
    high_ref, low_ref = near_refs[:2]
    dims = (((1,), (0,)), ((), ()))
    put_nodes(nodes, 0, node_values(int_ref[...], dims, high_ref, low_ref))
    put_nodes(nodes, int_ref.shape[1], node_values(if_ref[...], dims, high_ref, low_ref))
    for fetch in fetches[2:]:
        fetch.wait()


def half_of(own, halo):
    return up(up(own, 128) + up(halo, 128), 256) // 2


def prepare(u_int, u_if, halo, arrays):
    half = up(half_of(u_int.shape[1] + u_if.shape[1], halo), 128)
    vmem = pl.BlockSpec(memory_space=pltpu.VMEM)
    return pl.pallas_call(
        prepare_kernel,
        in_specs=[vmem] * 2 + [pl.BlockSpec(memory_space=pl.ANY)] * len(arrays),
        out_specs=[vmem] * (1 + len(arrays)),
        scratch_shapes=[pltpu.SemaphoreType.DMA((len(arrays),))],
        out_shape=[pltpu.VMEM((4 * GROUPS * PART, half), BF16)] + [pltpu.VMEM(x.shape, x.dtype) for x in arrays],
        compiler_params=pltpu.CompilerParams(vmem_limit_bytes=56 << 20),
        cost_estimate=lasts(5),
        name="own_nodes",
    )(u_int, u_if, *arrays)


def element_kernel(*refs, neighbours, chunk, own, half, kept):
    refs = list(refs)

    def take(n):
        taken, refs[:n] = refs[:n], []
        return taken

    count_ref, base_ref = take(2)
    halo_refs = take(neighbours)
    conn_ref, size_ref, stiff_ref, yield_ref, rate_ref, init_ref = take(6)
    high_ref, low_ref, strain_ref, force_ref = take(4)
    far_refs = take(kept)
    end_ref, pint_ref, pif_ref = take(3)
    back_refs = take(neighbours)
    near_refs = take(kept)
    nodes, onehot, corners, forces, state, total, arrived = refs
    fetches = [
        pltpu.make_async_copy(far, near, arrived.at[k]) for k, (far, near) in enumerate(zip(far_refs, near_refs))
    ]
    for fetch in fetches:
        fetch.start()
    n_int, n_if, slots = pint_ref.shape[0], pif_ref.shape[0], halo_refs[0].shape[0]
    halo_at = up(own, 128)
    both = 2 * GROUPS * PART
    chunks = end_ref.shape[1] // chunk
    count = count_ref[0]
    used = jnp.maximum(lax.div(count + chunk - 1, chunk), 1)

    total[...] = jnp.zeros_like(total)
    nodes[...] = base_ref[...]
    halo = jnp.concatenate([ref[...].astype(F32) for ref in halo_refs], axis=0).astype(BF16)
    put_nodes(nodes, halo_at, node_values(halo, NT, high_ref, low_ref))

    def columns(c):
        return pl.ds(pl.multiple_of(c * chunk, chunk), chunk)

    def place(c, corner):
        node = conn_ref[pl.ds(corner, 1), columns(c)]
        node = node + jnp.where(node >= own, halo_at - own, 0)
        upper = node >= half
        return upper, node - jnp.where(upper, half, 0)

    def gather(c, corner):
        upper, node = place(c, corner)
        hot = jnp.where(lax.broadcasted_iota(jnp.int32, (half, chunk), 0) == node, 1.0, 0.0).astype(BF16)
        onehot[lax.rem(c, 3), corner] = hot
        found = jnp.dot(nodes[...], hot, preferred_element_type=F32)
        found = jnp.where(upper, found[both:], found[:both])
        rows = pl.ds(pl.multiple_of(corner * 2 * PART, 8), 2 * PART)
        for group in range(GROUPS):
            corners[lax.rem(c, 2), group, rows, :] = found[group * 2 * PART : (group + 1) * 2 * PART]

    def alive(c):
        slot = c * chunk + lax.broadcasted_iota(jnp.int32, (1, chunk), 1)
        return jnp.where(slot < count, 1.0, 0.0)

    def advance(c, group):
        at = columns(c)
        size, limit, rate = size_ref[:, at], yield_ref[:, at], rate_ref[:, at]
        modulus = stiff_ref[:, at] * (2.0 / size)

        def wide(row):
            return jnp.broadcast_to(row, (8, chunk))

        twice_shear, shear, lame = wide(modulus * (2.0 * SHEAR)), wide(modulus * SHEAR), wide(modulus * LAME)
        inverse, relax = wide(1.0 / limit), wide(rate * limit)
        scale = size * size * 0.25 * alive(c)
        corner_values = corners[lax.rem(c, 2), group].astype(BF16)
        delta = jnp.dot(strain_ref[...], corner_values, preferred_element_type=F32)
        stress = tuple(state[comp * 8 : comp * 8 + 8, :] for comp in range(6))
        history = []
        for step in range(STEPS):
            d = [delta[step * 48 + comp * 8 : step * 48 + comp * 8 + 8] for comp in range(6)]
            trace = lame * (d[0] + d[1] + d[2])
            stress = tuple(
                s + (twice_shear * d[comp] + trace if comp < 3 else shear * d[comp]) - relax * jnp.tanh(s * inverse)
                for comp, s in enumerate(stress)
            )
            history += list(stress)
        for comp in range(6):
            state[comp * 8 : comp * 8 + 8, :] = stress[comp]
        force = jnp.dot(force_ref[...], jnp.concatenate(history, axis=0).astype(BF16), preferred_element_type=F32)
        force = (force * scale).astype(BF16)
        rows = pl.ds(pl.multiple_of(group * SLOT, SLOT), SLOT)
        for corner in range(8):
            forces[lax.rem(c, 2), corner, rows, :] = force[corner * SLOT : (corner + 1) * SLOT]

    def scatter(c, corner):
        upper, _ = place(c, corner)
        part = forces[lax.rem(c, 2), corner].astype(F32)
        part = jnp.concatenate([jnp.where(upper, 0.0, part), jnp.where(upper, part, 0.0)], axis=0).astype(BF16)
        total[...] += lax.dot_general(onehot[lax.rem(c, 3), corner], part, NT, preferred_element_type=F32)

    turns = 8

    def stage(c, first, middle, last):
        if middle:
            state[...] = init_ref[:, columns(c)]

        @pl.loop(0, 8, step=turns)
        def _(turn):
            for k in range(turns) if last else ():
                scatter(c - 1, turn + k)
            for k in range(turns) if middle else ():
                advance(c, turn + k)
            for k in range(turns) if first else ():
                gather(c + 1, turn + k)

        if middle:
            end_ref[:, columns(c)] = state[...] * alive(c)

    stage(-1, True, False, False)

    @pl.when(used > 1)
    def _():
        stage(0, True, True, False)

        @pl.loop(1, used - 1)
        def _(c):
            stage(c, True, True, True)

        stage(used - 1, False, True, True)

    @pl.when(used == 1)
    def _():
        stage(0, False, True, False)

    stage(used, False, False, True)

    @pl.loop(used, chunks)
    def _(c):
        end_ref[:, columns(c)] = jnp.zeros((end_ref.shape[0], chunk), F32)

    def result(start, length):
        cut = min(max(half - start, 0), length)
        runs = []
        if cut:
            runs.append(total[start : start + cut, :ROWS])
        if cut < length:
            runs.append(total[start + cut - half : start + length - half, ROWS:])
        return runs[0] if len(runs) == 1 else jnp.concatenate(runs, axis=0)

    pint_ref[...] = result(0, n_int)
    pif_ref[...] = result(n_int, n_if)
    for slot_index, back_ref in enumerate(back_refs):
        back_ref[...] = result(halo_at + slot_index * slots, slots)
    for fetch in fetches:
        fetch.wait()


def whole(shape):
    return pl.BlockSpec(shape, lambda *_: (0,) * len(shape))


def element_phase(count, nodes, halos, sizes, conn, params, stress_init, tables, later=()):
    chunk = 256
    n_int, n_if = sizes
    own = n_int + n_if
    neighbours, slots = len(halos), halos[0].shape[0]
    half = nodes.shape[1]
    vmem = pl.BlockSpec(memory_space=pltpu.VMEM)
    inputs = [nodes, *halos, conn, *params, stress_init, *tables]
    return pl.pallas_call(
        functools.partial(element_kernel, neighbours=neighbours, chunk=chunk, own=own, half=half, kept=len(later)),
        in_specs=[pl.BlockSpec(memory_space=pltpu.SMEM)] + [vmem] * len(inputs)
        + [pl.BlockSpec(memory_space=pl.ANY)] * len(later),
        out_specs=[vmem] * (3 + neighbours + len(later)),
        scratch_shapes=[
            pltpu.VMEM((4 * GROUPS * PART, half), BF16),
            pltpu.VMEM((3, 8, half, chunk), BF16),
            pltpu.VMEM((2, GROUPS, 16 * PART, chunk), F32),
            pltpu.VMEM((2, 8, ROWS, chunk), BF16),
            pltpu.VMEM((stress_init.shape[0], chunk), F32),
            pltpu.VMEM((half, 2 * ROWS), F32),
            pltpu.SemaphoreType.DMA((max(len(later), 1),)),
        ],
        out_shape=[
            jax.ShapeDtypeStruct(stress_init.shape, F32),
            pltpu.VMEM((n_int, ROWS), F32),
            pltpu.VMEM((n_if, ROWS), F32),
        ]
        + [pltpu.VMEM((slots, ROWS), F32)] * neighbours
        + [pltpu.VMEM(x.shape, x.dtype) for x in later],
        compiler_params=pltpu.CompilerParams(vmem_limit_bytes=LIMIT << 20),
        cost_estimate=lasts(40),
        name="elements",
    )(count, *inputs, *later)


def send_kernel(int_ref, if_ref, map_ref, *out_refs):
    n_int, n_if = int_ref.shape[1], if_ref.shape[1]
    slots = map_ref.shape[1]
    for slot_index, out_ref in enumerate(out_refs):
        wanted = map_ref[slot_index : slot_index + 1, :]
        rows = None
        for first, ref in ((0, int_ref), (n_int, if_ref)):
            hot = lax.broadcasted_iota(jnp.int32, (ref.shape[1], slots), 0) + first == wanted
            hot = jnp.where(hot, 1.0, 0.0).astype(BF16)
            found = jnp.dot(ref[...], hot, preferred_element_type=F32)
            rows = found if rows is None else rows + found
        out_ref[...] = rows.T.astype(BF16)


def send_blocks(u_int, u_if, send_map):
    neighbours, slots = send_map.shape
    return pl.pallas_call(
        send_kernel,
        out_shape=[jax.ShapeDtypeStruct((slots, u_int.shape[0]), BF16)] * neighbours,
        compiler_params=pltpu.CompilerParams(vmem_limit_bytes=60 << 20), cost_estimate=lasts(3), name="halo_rows",
    )(u_int, u_if, send_map)


def added_back(own, map_ref, returned, first):
    for slot_index, ref in enumerate(returned):
        hot = (
            lax.broadcasted_iota(jnp.int32, (own.shape[0], ref.shape[0]), 0) + first
            == map_ref[slot_index : slot_index + 1, :]
        )
        hot = jnp.where(hot, 1.0, 0.0).astype(BF16)
        value = ref[...]
        high = value.astype(BF16)
        low = (value - high.astype(F32)).astype(BF16)
        own = own + jnp.dot(hot, high, preferred_element_type=F32) + jnp.dot(hot, low, preferred_element_type=F32)
    return own


def interface_kernel(own_ref, map_ref, *refs, first):
    returned, outs = refs[:-4], refs[-4:]
    value = added_back(own_ref[...], map_ref, returned, first)
    half = outs[0].shape[0]
    for part, rows in enumerate((value[:half], value[half:])):
        outs[part][...] = rows
        outs[2 + part][...] = rows.astype(BF16)


def join_kernel(own_a, got_a, own_b, got_b, a_ref, b_ref, sent_a, sent_b):
    for own, got, ref, sent in ((own_a, got_a, a_ref, sent_a), (own_b, got_b, b_ref, sent_b)):
        value = own[...] + got[...].astype(F32)
        ref[...] = value
        sent[...] = value.astype(BF16)


def halves(n_rows):
    sizes = (n_rows // 2, n_rows - n_rows // 2)
    return [jax.ShapeDtypeStruct((size, ROWS), kind) for kind in (F32, BF16) for size in sizes]


def interleaved(value, scratch):
    nodes, width = value.shape
    fourier = width // 3
    for comp in range(3):
        scratch[pl.ds(comp, nodes, stride=3), :] = value[:, comp * fourier : (comp + 1) * fourier]
    return scratch[...]


def separated(value, scratch):
    scratch[...] = value
    nodes = value.shape[0] // 3
    return jnp.concatenate([scratch[pl.ds(comp, nodes, stride=3), :] for comp in range(3)], axis=1)


def interior_rhs_kernel(own_ref, map_ref, *refs):
    returned = refs[:-4]
    load_ref, anal_ref, rhs_ref, scratch = refs[-4:]
    value = added_back(own_ref[...], map_ref, returned, 0)
    force = jnp.dot(value, anal_ref[...], precision=HIGHEST, preferred_element_type=F32)
    rhs_ref[...] = interleaved(load_ref[...].T - force, scratch).astype(BF16)


def interior_kernel(rhs_ref, kinv_ref, du_ref, scratch):
    du = jnp.dot(kinv_ref[...], rhs_ref[...], preferred_element_type=F32)
    du_ref[...] = separated(du, scratch).T


def solve_kernel(load_ref, own_a, got_a, own_b, got_b, anal_ref, sinv_ref, *refs, peers):
    away_ref, near_ref, scratch, total, rows = refs
    depth_all = sinv_ref.shape[0]
    blocks = next(b for b in (4, 3, 2, 1) if b == 1 or depth_all % (b * 16) == 0)
    depth = depth_all // blocks
    value = jnp.concatenate([own_a[...] + got_a[...].astype(F32), own_b[...] + got_b[...].astype(F32)], axis=0)
    force = jnp.dot(value, anal_ref[...], precision=HIGHEST, preferred_element_type=F32)
    right = interleaved(load_ref[...].T - force, scratch).T.astype(BF16)
    for k in range(blocks):
        part = slice(k * depth, (k + 1) * depth)
        term = jnp.dot(right[:, part], sinv_ref[part, :], preferred_element_type=F32)
        total[...] = term if k == 0 else total[...] + term
    rows[...] = total[...].T
    count = rows.shape[0] // peers
    me = lax.axis_index("dom")
    for j in range(peers):
        at = (me ^ j) * count
        upper, lower = rows[pl.ds(at, count // 2), :], rows[pl.ds(at + count // 2, count // 2), :]
        out_ref = away_ref if j & 1 else near_ref
        out_ref[j // 2] = jnp.concatenate([upper, lower], axis=1).astype(out_ref.dtype)


def interface_solve(load, own_a, got_a, own_b, got_b, analysis, sinv, peers):
    depth, rows = sinv.shape
    fourier = load.shape[0] // 3
    shape = (peers // 2, rows // peers // 2, 2 * fourier)
    vmem = pl.BlockSpec(memory_space=pltpu.VMEM)
    small = [load, own_a, got_a, own_b, got_b, analysis]
    return pl.pallas_call(
        functools.partial(solve_kernel, peers=peers),
        in_specs=[vmem] * (len(small) + 1),
        out_specs=[vmem] * 2,
        scratch_shapes=[
            pltpu.VMEM((depth, fourier), F32),
            pltpu.VMEM((fourier, rows), F32),
            pltpu.VMEM((rows, fourier), F32),
        ],
        out_shape=[jax.ShapeDtypeStruct(shape, BF16), jax.ShapeDtypeStruct(shape, F32)],
        compiler_params=pltpu.CompilerParams(vmem_limit_bytes=12 << 20),
        cost_estimate=lasts(10),
        name="interface_solve",
    )(*small, sinv)


def split_kernel(mine_ref, got_ref, *outs):
    keep_ref, sent = outs[0], outs[1:]
    for j in range(mine_ref.shape[0]):
        value = mine_ref[j] + got_ref[j].astype(F32)
        if len(sent) == 1:
            ref = sent[0] if j & 1 else keep_ref
            ref[j // 2] = value.astype(ref.dtype)
        elif j == 0:
            keep_ref[...] = value
        else:
            sent[j - 1][...] = value.astype(BF16)


def split(mine, got, apart):
    count, shape = mine.shape[0], mine.shape[1:]
    if apart:
        outs = [jax.ShapeDtypeStruct(shape, F32)] + [jax.ShapeDtypeStruct(shape, BF16)] * (count - 1)
    else:
        outs = [jax.ShapeDtypeStruct((count // 2, *shape), kind) for kind in (F32, BF16)]
    return pl.pallas_call(split_kernel, out_shape=outs, compiler_params=SMALL, cost_estimate=lasts(4), name="correction_sums")(mine, got)


def last_kernel(mine_ref, *refs):
    got_refs, (out_ref, scratch) = refs[:-2], refs[-2:]
    value = mine_ref[...]
    for ref in got_refs:
        value = value + ref[...].astype(F32)
    fourier = value.shape[1] // 2
    out_ref[...] = separated(jnp.concatenate([value[:, :fourier], value[:, fourier:]], axis=0), scratch)


def swapped(shard, axis, bit):
    peers = lax.axis_size(axis)
    return lax.ppermute(shard, axis, [(i, i ^ bit) for i in range(peers)])


def passed_along(shard, axis, by):
    peers = lax.axis_size(axis)
    return lax.ppermute(shard, axis, [(i, (i + by) % peers) for i in range(peers)])


def per_device(
    u_int,
    u_if,
    load_int,
    load_if,
    conn,
    send_map,
    counts,
    elem_size,
    stiffness,
    yield_stress,
    relax_rate,
    stress_init,
    kinv_int,
    sinv,
):
    width = u_int.shape[1]
    fourier = width // 3
    n_int, n_if = u_int.shape[0], u_if.shape[0]
    neighbours, slots = send_map.shape
    reach = neighbours // 2
    offsets = list(range(-reach, 0)) + list(range(1, reach + 1))
    tables = constants(fourier)
    analysis = tables[4]

    blocks = send_blocks(u_int.T, u_if.T, send_map)
    halos = [passed_along(blocks[j], "dom", offsets[j]) for j in range(neighbours)]
    params = [x.reshape(1, -1) for x in (elem_size, stiffness, yield_stress, relax_rate)]
    later = (sinv.T, kinv_int, load_int.T, load_if.T, analysis, send_map)
    nodes, synth_high, synth_low, strain, force, near_conn, init, *params = (
        pltpu.with_memory_space_constraint(x, pltpu.VMEM)
        for x in prepare(u_int.T, u_if.T, neighbours * slots, [*tables[:4], conn.T, stress_init, *params])
    )
    stress_end, p_int, p_if, *more = element_phase(
        counts,
        nodes,
        halos,
        (n_int, n_if),
        near_conn,
        params,
        init,
        (synth_high, synth_low, strain, force),
        later,
    )
    back = more[:neighbours]
    sinv_t, kinv, load_int_t, load_if_t, analysis, near_map = (
        pltpu.with_memory_space_constraint(x, pltpu.VMEM) for x in more[neighbours:]
    )
    returned = [passed_along(back[j], "dom", -offsets[j]) for j in range(neighbours)]

    part_a, part_b, sent_a, sent_b = pl.pallas_call(
        functools.partial(interface_kernel, first=n_int), out_shape=halves(n_if), compiler_params=SMALL, cost_estimate=lasts(4), name="interface_forces"
    )(p_if, near_map, *returned)

    rhs_int = pl.pallas_call(
        interior_rhs_kernel,
        out_shape=jax.ShapeDtypeStruct((3 * n_int, fourier), BF16),
        scratch_shapes=[pltpu.VMEM((3 * n_int, fourier), F32)],
        compiler_params=SMALL, cost_estimate=lasts(12), name="interior_rhs",
    )(p_int, near_map, *returned, load_int_t, analysis)

    bits = [1 << b for b in range(lax.axis_size("grp").bit_length() - 1)]
    for turn, (bit_a, bit_b) in enumerate(zip(bits, bits[::-1])):
        if turn:
            part_a, part_b, sent_a, sent_b = pl.pallas_call(
                join_kernel, out_shape=halves(n_if), compiler_params=SMALL, cost_estimate=lasts(5), name="interface_sums"
            )(part_a, got_a, part_b, got_b)
            sent_a, sent_b, rhs_int = lax.optimization_barrier((sent_a, sent_b, rhs_int))
        got_a, got_b = swapped(sent_a, "grp", bit_a), swapped(sent_b, "grp", bit_b)

    du_int = pl.pallas_call(
        interior_kernel,
        out_shape=jax.ShapeDtypeStruct((width, n_int), F32),
        scratch_shapes=[pltpu.VMEM((3 * n_int, fourier), F32)],
        compiler_params=SMALL, cost_estimate=lasts(6), name="interior_solve",
    )(rhs_int, kinv).T

    peers = lax.axis_size("dom")
    sent, mine = interface_solve(load_if_t, part_a, got_a, part_b, got_b, analysis, sinv_t, peers)
    bit = 1
    while True:
        got = swapped(sent, "dom", bit)
        apart = mine.shape[0] <= 4
        mine, *sent = split(mine, got, apart)
        bit *= 2
        if apart:
            break
        sent = sent[0]
    got = [swapped(block, "dom", bit * (j + 1)) for j, block in enumerate(sent)]
    rows = sinv.shape[0] // peers
    du_if = pl.pallas_call(
        last_kernel,
        out_shape=jax.ShapeDtypeStruct((rows // 3, width), F32),
        scratch_shapes=[pltpu.VMEM((rows, fourier), F32)],
        compiler_params=SMALL, cost_estimate=lasts(2), name="interface_result",
    )(mine, *got)
    return (du_int, du_if, stress_end)


def solution(mesh):
    return jax.shard_map(
        per_device,
        mesh=mesh,
        in_specs=(
            P(("grp", "dom"), None),
            P("dom", None),
            P(("grp", "dom"), None),
            P("dom", None),
            P(("grp", "dom"), None),
            P(("grp", "dom"), None),
            P(("grp", "dom")),
            P(("grp", "dom")),
            P(("grp", "dom")),
            P(("grp", "dom")),
            P(("grp", "dom")),
            P(None, ("grp", "dom")),
            P(("grp", "dom"), None),
            P("grp", "dom"),
        ),
        out_specs=(P(("grp", "dom"), None), P(("grp", "dom"), None), P(None, ("grp", "dom"))),
        check_vma=False,
    )
```

```python
import functools
import math

import jax
import jax.numpy as jnp
import numpy as np
from jax import lax
from jax.experimental import pallas as pl
from jax.experimental.pallas import tpu as pltpu
from jax.sharding import PartitionSpec as P

TIMES = 32
POISSON = 0.3
LAME = POISSON / ((1.0 + POISSON) * (1.0 - 2.0 * POISSON))
SHEAR = 1.0 / (2.0 * (1.0 + POISSON))
HIGHEST = lax.Precision.HIGHEST
STEPS = 4
GROUPS = TIMES // STEPS
PART = 3 * STEPS
SLOT = 16
ROWS = GROUPS * SLOT
NT = (((1,), (1,)), ((), ()))


def lasts(microseconds):
    return pl.CostEstimate(flops=0, bytes_accessed=int(3e6 * microseconds), transcendentals=0)


LIMIT = 30
SMALL = pltpu.CompilerParams(vmem_limit_bytes=12 << 20)
BF16 = jnp.bfloat16
F32 = jnp.float32


def strain_table():
    gauss = 1.0 / math.sqrt(3.0)
    table = np.zeros((6, 8, 8, 3))
    for point in range(8):
        coords = [((point >> bit & 1) * 2 - 1) * gauss for bit in range(3)]
        for corner in range(8):
            signs = [(corner >> bit & 1) * 2 - 1 for bit in range(3)]
            deriv = []
            for axis in range(3):
                value = signs[axis] / 8.0
                for other in range(3):
                    if other != axis:
                        value = value * (1.0 + signs[other] * coords[other])
                deriv.append(value)
            table[0, point, corner, 0] = deriv[0]
            table[1, point, corner, 1] = deriv[1]
            table[2, point, corner, 2] = deriv[2]
            table[3, point, corner, 0] = deriv[1]
            table[3, point, corner, 1] = deriv[0]
            table[4, point, corner, 1] = deriv[2]
            table[4, point, corner, 2] = deriv[1]
            table[5, point, corner, 2] = deriv[0]
            table[5, point, corner, 0] = deriv[2]
    return table.reshape(48, 24).astype(np.float32)


def time_tables(fourier):
    theta = 2.0 * math.pi * (np.arange(TIMES) + 0.3) / TIMES
    synthesis = np.zeros((fourier, TIMES))
    for column in range(fourier):
        harmonic = column // 2
        if column % 2 == 0:
            synthesis[column] = np.cos(harmonic * theta)
        else:
            synthesis[column] = np.sin((harmonic + 1) * theta)
    analysis = synthesis.T * (2.0 / TIMES)
    analysis[:, 0] = 1.0 / TIMES
    return synthesis.astype(np.float32), analysis.astype(np.float32)


def constants(fourier):
    synthesis, analysis = time_tables(fourier)
    differences = synthesis.astype(np.float64) - np.roll(synthesis.astype(np.float64), 1, axis=1)
    synth = np.zeros((GROUPS, 2, 3, STEPS, 3, fourier))
    anal = np.zeros((GROUPS, SLOT, 3, fourier))
    for comp in range(3):
        synth[:, :, comp, :, comp, :] = differences.T.reshape(GROUPS, 1, STEPS, fourier)
        anal[:, comp * STEPS : (comp + 1) * STEPS, comp, :] = analysis.reshape(GROUPS, STEPS, fourier)
    synth = jnp.asarray(synth.reshape(2 * GROUPS * PART, 3 * fourier), F32)
    table = strain_table().reshape(48, 8, 3)
    strain = np.zeros((STEPS, 48, 8, 2, 3, STEPS), np.float32)
    force = np.zeros((8, SLOT, STEPS, 48), np.float32)
    for step in range(STEPS):
        for half in range(2):
            strain[step, :, :, half, :, step] = table
        for comp in range(3):
            force[:, comp * STEPS + step, step, :] = table[:, :, comp].T
    high = synth.astype(BF16)
    low = (synth - high.astype(F32)).astype(BF16)
    return (
        high,
        low,
        jnp.asarray(strain.reshape(STEPS * 48, 16 * PART)).astype(BF16),
        jnp.asarray(force.reshape(8 * SLOT, STEPS * 48)).astype(BF16),
        jnp.asarray(anal.reshape(ROWS, 3 * fourier), F32),
        jnp.asarray(anal[:, :PART].reshape(GROUPS * PART, 3 * fourier), F32),
    )


def up(n, to):
    return -(-n // to) * to


def node_values(rows, dims, high_ref, low_ref):
    value = lax.dot_general(high_ref[...], rows, dims, preferred_element_type=F32)
    value = value + lax.dot_general(low_ref[...], rows, dims, preferred_element_type=F32)
    upper = value.astype(BF16).astype(F32)
    row = lax.broadcasted_iota(jnp.int32, (value.shape[0], 1), 0)
    return jnp.where(lax.rem(row, 2 * PART) < PART, upper, value - upper).astype(BF16)


def put_nodes(nodes, start, value):
    both, half, length = nodes.shape[0] // 2, nodes.shape[1], value.shape[1]
    cut = min(max(half - start, 0), length)
    if cut:
        nodes[:both, start : start + cut] = value[:, :cut]
    if cut < length:
        at = start + cut - half
        nodes[both:, at : at + length - cut] = value[:, cut:]


def prepare_kernel(int_ref, if_ref, *refs):
    kept = len(refs) // 2 - 1
    far_refs, nodes, near_refs, arrived = refs[:kept], refs[kept], refs[kept + 1 : -1], refs[-1]
    fetches = [
        pltpu.make_async_copy(far, near, arrived.at[k]) for k, (far, near) in enumerate(zip(far_refs, near_refs))
    ]
    for fetch in fetches:
        fetch.start()
    nodes[...] = jnp.zeros_like(nodes)
    for fetch in fetches[:2]:
        fetch.wait()
    high_ref, low_ref = near_refs[:2]
    dims = (((1,), (0,)), ((), ()))
    put_nodes(nodes, 0, node_values(int_ref[...], dims, high_ref, low_ref))
    put_nodes(nodes, int_ref.shape[1], node_values(if_ref[...], dims, high_ref, low_ref))
    for fetch in fetches[2:]:
        fetch.wait()


def half_of(own, halo):
    return up(up(own, 128) + up(halo, 128), 256) // 2


def prepare(u_int, u_if, halo, arrays):
    half = up(half_of(u_int.shape[1] + u_if.shape[1], halo), 128)
    vmem = pl.BlockSpec(memory_space=pltpu.VMEM)
    return pl.pallas_call(
        prepare_kernel,
        in_specs=[vmem] * 2 + [pl.BlockSpec(memory_space=pl.ANY)] * len(arrays),
        out_specs=[vmem] * (1 + len(arrays)),
        scratch_shapes=[pltpu.SemaphoreType.DMA((len(arrays),))],
        out_shape=[pltpu.VMEM((4 * GROUPS * PART, half), BF16)] + [pltpu.VMEM(x.shape, x.dtype) for x in arrays],
        compiler_params=pltpu.CompilerParams(vmem_limit_bytes=56 << 20),
        cost_estimate=lasts(5),
        name="own_nodes",
    )(u_int, u_if, *arrays)


def element_kernel(*refs, neighbours, chunk, own, half, kept):
    refs = list(refs)

    def take(n):
        taken, refs[:n] = refs[:n], []
        return taken

    count_ref, base_ref = take(2)
    halo_refs = take(neighbours)
    conn_ref, size_ref, stiff_ref, yield_ref, rate_ref, init_ref = take(6)
    high_ref, low_ref, strain_ref, force_ref = take(4)
    far_refs = take(kept)
    end_ref, pint_ref, pif_ref = take(3)
    back_refs = take(neighbours)
    near_refs = take(kept)
    nodes, onehot, corners, forces, state, total, arrived = refs
    fetches = [
        pltpu.make_async_copy(far, near, arrived.at[k]) for k, (far, near) in enumerate(zip(far_refs, near_refs))
    ]
    for fetch in fetches:
        fetch.start()
    n_int, n_if, slots = pint_ref.shape[0], pif_ref.shape[0], halo_refs[0].shape[0]
    halo_at = up(own, 128)
    both = 2 * GROUPS * PART
    chunks = end_ref.shape[1] // chunk
    count = count_ref[0]
    used = jnp.maximum(lax.div(count + chunk - 1, chunk), 1)

    total[...] = jnp.zeros_like(total)
    nodes[...] = base_ref[...]
    halo = jnp.concatenate([ref[...].astype(F32) for ref in halo_refs], axis=0).astype(BF16)
    put_nodes(nodes, halo_at, node_values(halo, NT, high_ref, low_ref))

    def columns(c):
        return pl.ds(pl.multiple_of(c * chunk, chunk), chunk)

    def place(c, corner):
        node = conn_ref[pl.ds(corner, 1), columns(c)]
        node = node + jnp.where(node >= own, halo_at - own, 0)
        upper = node >= half
        return upper, node - jnp.where(upper, half, 0)

    def gather(c, corner):
        upper, node = place(c, corner)
        hot = jnp.where(lax.broadcasted_iota(jnp.int32, (half, chunk), 0) == node, 1.0, 0.0).astype(BF16)
        onehot[lax.rem(c, 3), corner] = hot
        found = jnp.dot(nodes[...], hot, preferred_element_type=F32)
        found = jnp.where(upper, found[both:], found[:both])
        rows = pl.ds(pl.multiple_of(corner * 2 * PART, 8), 2 * PART)
        for group in range(GROUPS):
            corners[lax.rem(c, 2), group, rows, :] = found[group * 2 * PART : (group + 1) * 2 * PART]

    def alive(c):
        slot = c * chunk + lax.broadcasted_iota(jnp.int32, (1, chunk), 1)
        return jnp.where(slot < count, 1.0, 0.0)

    def advance(c, group):
        at = columns(c)
        size, limit, rate = size_ref[:, at], yield_ref[:, at], rate_ref[:, at]
        modulus = stiff_ref[:, at] * (2.0 / size)

        def wide(row):
            return jnp.broadcast_to(row, (8, chunk))

        twice_shear, shear, lame = wide(modulus * (2.0 * SHEAR)), wide(modulus * SHEAR), wide(modulus * LAME)
        inverse, relax = wide(1.0 / limit), wide(rate * limit)
        scale = size * size * 0.25 * alive(c)
        corner_values = corners[lax.rem(c, 2), group].astype(BF16)
        delta = jnp.dot(strain_ref[...], corner_values, preferred_element_type=F32)
        stress = tuple(state[comp * 8 : comp * 8 + 8, :] for comp in range(6))
        history = []
        for step in range(STEPS):
            d = [delta[step * 48 + comp * 8 : step * 48 + comp * 8 + 8] for comp in range(6)]
            trace = lame * (d[0] + d[1] + d[2])
            stress = tuple(
                s + (twice_shear * d[comp] + trace if comp < 3 else shear * d[comp]) - relax * jnp.tanh(s * inverse)
                for comp, s in enumerate(stress)
            )
            history += list(stress)
        for comp in range(6):
            state[comp * 8 : comp * 8 + 8, :] = stress[comp]
        force = jnp.dot(force_ref[...], jnp.concatenate(history, axis=0).astype(BF16), preferred_element_type=F32)
        force = (force * scale).astype(BF16)
        rows = pl.ds(pl.multiple_of(group * SLOT, SLOT), SLOT)
        for corner in range(8):
            forces[lax.rem(c, 2), corner, rows, :] = force[corner * SLOT : (corner + 1) * SLOT]

    def scatter(c, corner):
        upper, _ = place(c, corner)
        part = forces[lax.rem(c, 2), corner].astype(F32)
        part = jnp.concatenate([jnp.where(upper, 0.0, part), jnp.where(upper, part, 0.0)], axis=0).astype(BF16)
        total[...] += lax.dot_general(onehot[lax.rem(c, 3), corner], part, NT, preferred_element_type=F32)

    turns = 8

    def stage(c, first, middle, last):
        if middle:
            state[...] = init_ref[:, columns(c)]

        @pl.loop(0, 8, step=turns)
        def _(turn):
            for k in range(turns) if last else ():
                scatter(c - 1, turn + k)
            for k in range(turns) if middle else ():
                advance(c, turn + k)
            for k in range(turns) if first else ():
                gather(c + 1, turn + k)

        if middle:
            end_ref[:, columns(c)] = state[...] * alive(c)

    stage(-1, True, False, False)

    @pl.when(used > 1)
    def _():
        stage(0, True, True, False)

        @pl.loop(1, used - 1)
        def _(c):
            stage(c, True, True, True)

        stage(used - 1, False, True, True)

    @pl.when(used == 1)
    def _():
        stage(0, False, True, False)

    stage(used, False, False, True)

    @pl.loop(used, chunks)
    def _(c):
        end_ref[:, columns(c)] = jnp.zeros((end_ref.shape[0], chunk), F32)

    def result(start, length):
        cut = min(max(half - start, 0), length)
        runs = []
        if cut:
            runs.append(total[start : start + cut, :ROWS])
        if cut < length:
            runs.append(total[start + cut - half : start + length - half, ROWS:])
        return runs[0] if len(runs) == 1 else jnp.concatenate(runs, axis=0)

    pint_ref[...] = result(0, n_int)
    pif_ref[...] = result(n_int, n_if)
    for slot_index, back_ref in enumerate(back_refs):
        back_ref[...] = result(halo_at + slot_index * slots, slots)
    for fetch in fetches:
        fetch.wait()


def whole(shape):
    return pl.BlockSpec(shape, lambda *_: (0,) * len(shape))


def element_phase(count, nodes, halos, sizes, conn, params, stress_init, tables, later=()):
    chunk = 256
    n_int, n_if = sizes
    own = n_int + n_if
    neighbours, slots = len(halos), halos[0].shape[0]
    half = nodes.shape[1]
    vmem = pl.BlockSpec(memory_space=pltpu.VMEM)
    inputs = [nodes, *halos, conn, *params, stress_init, *tables]
    return pl.pallas_call(
        functools.partial(element_kernel, neighbours=neighbours, chunk=chunk, own=own, half=half, kept=len(later)),
        in_specs=[pl.BlockSpec(memory_space=pltpu.SMEM)] + [vmem] * len(inputs)
        + [pl.BlockSpec(memory_space=pl.ANY)] * len(later),
        out_specs=[vmem] * (3 + neighbours + len(later)),
        scratch_shapes=[
            pltpu.VMEM((4 * GROUPS * PART, half), BF16),
            pltpu.VMEM((3, 8, half, chunk), BF16),
            pltpu.VMEM((2, GROUPS, 16 * PART, chunk), F32),
            pltpu.VMEM((2, 8, ROWS, chunk), BF16),
            pltpu.VMEM((stress_init.shape[0], chunk), F32),
            pltpu.VMEM((half, 2 * ROWS), F32),
            pltpu.SemaphoreType.DMA((max(len(later), 1),)),
        ],
        out_shape=[
            jax.ShapeDtypeStruct(stress_init.shape, F32),
            pltpu.VMEM((n_int, ROWS), F32),
            pltpu.VMEM((n_if, ROWS), F32),
        ]
        + [pltpu.VMEM((slots, ROWS), F32)] * neighbours
        + [pltpu.VMEM(x.shape, x.dtype) for x in later],
        compiler_params=pltpu.CompilerParams(vmem_limit_bytes=LIMIT << 20),
        cost_estimate=lasts(40),
        name="elements",
    )(count, *inputs, *later)


def send_kernel(int_ref, if_ref, map_ref, *out_refs):
    n_int, n_if = int_ref.shape[1], if_ref.shape[1]
    slots = map_ref.shape[1]
    for slot_index, out_ref in enumerate(out_refs):
        wanted = map_ref[slot_index : slot_index + 1, :]
        rows = None
        for first, ref in ((0, int_ref), (n_int, if_ref)):
            hot = lax.broadcasted_iota(jnp.int32, (ref.shape[1], slots), 0) + first == wanted
            hot = jnp.where(hot, 1.0, 0.0).astype(BF16)
            found = jnp.dot(ref[...], hot, preferred_element_type=F32)
            rows = found if rows is None else rows + found
        out_ref[...] = rows.T.astype(BF16)


def send_blocks(u_int, u_if, send_map):
    neighbours, slots = send_map.shape
    return pl.pallas_call(
        send_kernel,
        out_shape=[jax.ShapeDtypeStruct((slots, u_int.shape[0]), BF16)] * neighbours,
        compiler_params=pltpu.CompilerParams(vmem_limit_bytes=60 << 20), cost_estimate=lasts(3), name="halo_rows",
    )(u_int, u_if, send_map)


def added_back(own, map_ref, returned, first):
    for slot_index, ref in enumerate(returned):
        hot = (
            lax.broadcasted_iota(jnp.int32, (own.shape[0], ref.shape[0]), 0) + first
            == map_ref[slot_index : slot_index + 1, :]
        )
        hot = jnp.where(hot, 1.0, 0.0).astype(BF16)
        value = ref[...]
        high = value.astype(BF16)
        low = (value - high.astype(F32)).astype(BF16)
        own = own + jnp.dot(hot, high, preferred_element_type=F32) + jnp.dot(hot, low, preferred_element_type=F32)
    return own


def without_gaps(value):
    width = GROUPS * PART
    row = lax.broadcasted_iota(jnp.int32, (ROWS, width), 0)
    column = lax.broadcasted_iota(jnp.int32, (ROWS, width), 1)
    chosen = row == lax.div(column, PART) * SLOT + lax.rem(column, PART)
    value = jnp.dot(value.astype(BF16), jnp.where(chosen, 1.0, 0.0).astype(BF16), preferred_element_type=F32)
    tall = value.shape[0] // 4 * 3
    rest = jnp.concatenate([value[tall:, k * width // 3 : (k + 1) * width // 3] for k in range(3)], axis=0)
    return jnp.concatenate([value[:tall], rest], axis=1)


def with_rows_back(value):
    width = GROUPS * PART
    rest = value[:, width:]
    short = rest.shape[0] // 3
    rest = jnp.concatenate([rest[k * short : (k + 1) * short] for k in range(3)], axis=1)
    return jnp.concatenate([value[:, :width], rest], axis=0)


def interface_kernel(own_ref, map_ref, *refs, first):
    returned, (own_out, sent_out) = refs[:-2], refs[-2:]
    value = added_back(own_ref[...], map_ref, returned, first)
    upper = without_gaps(value)
    own_out[...] = upper + without_gaps(value - value.astype(BF16).astype(F32))
    sent_out[...] = upper.astype(BF16)


def interleaved(value, scratch):
    nodes, width = value.shape
    fourier = width // 3
    for comp in range(3):
        scratch[pl.ds(comp, nodes, stride=3), :] = value[:, comp * fourier : (comp + 1) * fourier]
    return scratch[...]


def separated(value, scratch):
    scratch[...] = value
    nodes = value.shape[0] // 3
    return jnp.concatenate([scratch[pl.ds(comp, nodes, stride=3), :] for comp in range(3)], axis=1)


def interior_rhs_kernel(own_ref, map_ref, *refs):
    returned = refs[:-4]
    load_ref, anal_ref, rhs_ref, scratch = refs[-4:]
    value = added_back(own_ref[...], map_ref, returned, 0)
    force = jnp.dot(value, anal_ref[...], precision=HIGHEST, preferred_element_type=F32)
    rhs_ref[...] = interleaved(load_ref[...].T - force, scratch).astype(BF16)


def interior_kernel(rhs_ref, kinv_ref, du_ref, scratch):
    du = jnp.dot(kinv_ref[...], rhs_ref[...], preferred_element_type=F32)
    du_ref[...] = separated(du, scratch).T


def solve_kernel(load_ref, anal_ref, own_ref, *refs, peers):
    got_refs, (sinv_ref, away_ref, near_ref, scratch, total, rows) = refs[:-6], refs[-6:]
    depth_all = sinv_ref.shape[0]
    blocks = next(b for b in (4, 3, 2, 1) if b == 1 or depth_all % (b * 16) == 0)
    depth = depth_all // blocks
    value = own_ref[...]
    for ref in got_refs:
        value = value + ref[...].astype(F32)
    force = jnp.dot(with_rows_back(value), anal_ref[...], precision=HIGHEST, preferred_element_type=F32)
    right = interleaved(load_ref[...].T - force, scratch).T.astype(BF16)
    for k in range(blocks):
        part = slice(k * depth, (k + 1) * depth)
        term = jnp.dot(right[:, part], sinv_ref[part, :], preferred_element_type=F32)
        total[...] = term if k == 0 else total[...] + term
    rows[...] = total[...].T
    count = rows.shape[0] // peers
    me = lax.axis_index("dom")
    for j in range(peers):
        at = (me ^ j) * count
        upper, lower = rows[pl.ds(at, count // 2), :], rows[pl.ds(at + count // 2, count // 2), :]
        out_ref = away_ref if j & 1 else near_ref
        out_ref[j // 2] = jnp.concatenate([upper, lower], axis=1).astype(out_ref.dtype)


def interface_solve(load, analysis, own, got, sinv, peers):
    depth, rows = sinv.shape
    fourier = load.shape[0] // 3
    shape = (peers // 2, rows // peers // 2, 2 * fourier)
    vmem = pl.BlockSpec(memory_space=pltpu.VMEM)
    small = [load, analysis, own, *got]
    return pl.pallas_call(
        functools.partial(solve_kernel, peers=peers),
        in_specs=[vmem] * (len(small) + 1),
        out_specs=[vmem] * 2,
        scratch_shapes=[
            pltpu.VMEM((depth, fourier), F32),
            pltpu.VMEM((fourier, rows), F32),
            pltpu.VMEM((rows, fourier), F32),
        ],
        out_shape=[jax.ShapeDtypeStruct(shape, BF16), jax.ShapeDtypeStruct(shape, F32)],
        compiler_params=pltpu.CompilerParams(vmem_limit_bytes=12 << 20),
        cost_estimate=lasts(10),
        name="interface_solve",
    )(*small, sinv)


def split_kernel(mine_ref, got_ref, *outs):
    keep_ref, sent = outs[0], outs[1:]
    for j in range(mine_ref.shape[0]):
        value = mine_ref[j] + got_ref[j].astype(F32)
        if len(sent) == 1:
            ref = sent[0] if j & 1 else keep_ref
            ref[j // 2] = value.astype(ref.dtype)
        elif j == 0:
            keep_ref[...] = value
        else:
            sent[j - 1][...] = value.astype(BF16)


def split(mine, got, apart):
    count, shape = mine.shape[0], mine.shape[1:]
    if apart:
        outs = [jax.ShapeDtypeStruct(shape, F32)] + [jax.ShapeDtypeStruct(shape, BF16)] * (count - 1)
    else:
        outs = [jax.ShapeDtypeStruct((count // 2, *shape), kind) for kind in (F32, BF16)]
    return pl.pallas_call(split_kernel, out_shape=outs, compiler_params=SMALL, cost_estimate=lasts(4), name="correction_sums")(mine, got)


def last_kernel(mine_ref, *refs):
    got_refs, (out_ref, scratch) = refs[:-2], refs[-2:]
    value = mine_ref[...]
    for ref in got_refs:
        value = value + ref[...].astype(F32)
    fourier = value.shape[1] // 2
    out_ref[...] = separated(jnp.concatenate([value[:, :fourier], value[:, fourier:]], axis=0), scratch)


def swapped(shard, axis, bit):
    peers = lax.axis_size(axis)
    return lax.ppermute(shard, axis, [(i, i ^ bit) for i in range(peers)])


def passed_along(shard, axis, by):
    peers = lax.axis_size(axis)
    return lax.ppermute(shard, axis, [(i, (i + by) % peers) for i in range(peers)])


def per_device(
    u_int,
    u_if,
    load_int,
    load_if,
    conn,
    send_map,
    counts,
    elem_size,
    stiffness,
    yield_stress,
    relax_rate,
    stress_init,
    kinv_int,
    sinv,
):
    width = u_int.shape[1]
    fourier = width // 3
    n_int, n_if = u_int.shape[0], u_if.shape[0]
    neighbours, slots = send_map.shape
    reach = neighbours // 2
    offsets = list(range(-reach, 0)) + list(range(1, reach + 1))
    tables = constants(fourier)
    analysis = tables[4]

    blocks = send_blocks(u_int.T, u_if.T, send_map)
    halos = [passed_along(blocks[j], "dom", offsets[j]) for j in range(neighbours)]
    params = [x.reshape(1, -1) for x in (elem_size, stiffness, yield_stress, relax_rate)]
    later = (sinv.T, kinv_int, load_int.T, load_if.T, analysis, send_map, tables[5])
    nodes, synth_high, synth_low, strain, force, near_conn, init, *params = (
        pltpu.with_memory_space_constraint(x, pltpu.VMEM)
        for x in prepare(u_int.T, u_if.T, neighbours * slots, [*tables[:4], conn.T, stress_init, *params])
    )
    stress_end, p_int, p_if, *more = element_phase(
        counts,
        nodes,
        halos,
        (n_int, n_if),
        near_conn,
        params,
        init,
        (synth_high, synth_low, strain, force),
        later,
    )
    back = more[:neighbours]
    sinv_t, kinv, load_int_t, load_if_t, analysis, near_map, compact = (
        pltpu.with_memory_space_constraint(x, pltpu.VMEM) for x in more[neighbours:]
    )
    returned = [passed_along(back[j], "dom", -offsets[j]) for j in range(neighbours)]

    packed = (n_if // 4 * 3, GROUPS * PART // 3 * 4)
    own_force, sent_force = pl.pallas_call(
        functools.partial(interface_kernel, first=n_int),
        out_shape=[jax.ShapeDtypeStruct(packed, kind) for kind in (F32, BF16)],
        compiler_params=SMALL,
        cost_estimate=lasts(1),
        name="interface_forces",
    )(p_if, near_map, *returned)
    got_force = [swapped(sent_force, "grp", other) for other in range(1, lax.axis_size("grp"))]

    rhs_int = pl.pallas_call(
        interior_rhs_kernel,
        out_shape=jax.ShapeDtypeStruct((3 * n_int, fourier), BF16),
        scratch_shapes=[pltpu.VMEM((3 * n_int, fourier), F32)],
        compiler_params=SMALL, cost_estimate=lasts(12), name="interior_rhs",
    )(p_int, near_map, *returned, load_int_t, analysis)

    du_int = pl.pallas_call(
        interior_kernel,
        out_shape=jax.ShapeDtypeStruct((width, n_int), F32),
        scratch_shapes=[pltpu.VMEM((3 * n_int, fourier), F32)],
        compiler_params=SMALL, cost_estimate=lasts(6), name="interior_solve",
    )(rhs_int, kinv).T

    peers = lax.axis_size("dom")
    sent, mine = interface_solve(load_if_t, compact, own_force, got_force, sinv_t, peers)
    bit = 1
    while True:
        got = swapped(sent, "dom", bit)
        apart = mine.shape[0] <= 4
        mine, *sent = split(mine, got, apart)
        bit *= 2
        if apart:
            break
        sent = sent[0]
    got = [swapped(block, "dom", bit * (j + 1)) for j, block in enumerate(sent)]
    rows = sinv.shape[0] // peers
    du_if = pl.pallas_call(
        last_kernel,
        out_shape=jax.ShapeDtypeStruct((rows // 3, width), F32),
        scratch_shapes=[pltpu.VMEM((rows, fourier), F32)],
        compiler_params=SMALL, cost_estimate=lasts(2), name="interface_result",
    )(mine, *got)
    return (du_int, du_if, stress_end)


def solution(mesh):
    return jax.shard_map(
        per_device,
        mesh=mesh,
        in_specs=(
            P(("grp", "dom"), None),
            P("dom", None),
            P(("grp", "dom"), None),
            P("dom", None),
            P(("grp", "dom"), None),
            P(("grp", "dom"), None),
            P(("grp", "dom")),
            P(("grp", "dom")),
            P(("grp", "dom")),
            P(("grp", "dom")),
            P(("grp", "dom")),
            P(None, ("grp", "dom")),
            P(("grp", "dom"), None),
            P("grp", "dom"),
        ),
        out_specs=(P(("grp", "dom"), None), P(("grp", "dom"), None), P(None, ("grp", "dom"))),
        check_vma=False,
    )
```
